512 devices in a mesh: dp: 16 (over y, core), ctx: 32 (over x, z).
Axes of the slice: x: 4, y: 8, z: 8, core: 2. Of those that a mesh axis runs over, the one named last changes fastest.
Arguments:
- mixer_input: bfloat16 [65536, 2560], P(('dp', 'ctx')), parts along dimension 0, may hold values from -6 to 6
- input_map: bfloat16 [65536, 128], P(('dp', 'ctx')), parts along dimension 0, may hold values from -6 to 6
- output_map: bfloat16 [65536, 128], P(('dp', 'ctx')), parts along dimension 0, may hold values from -0.015625 to 0.015625
- log_decay: float32 [65536, 40], P(('dp', 'ctx')), parts along dimension 0, may hold values from -1 to 0
- query_rows: bfloat16 [65536, 2560], P(('dp', 'ctx')), parts along dimension 0, may hold values from -7 to 7
- key_rows: bfloat16 [65536, 320], P(('dp', 'ctx')), parts along dimension 0, may hold values from -7 to 7
- value_rows: bfloat16 [65536, 320], P(('dp', 'ctx')), parts along dimension 0, may hold values from -6 to 6
Outputs:
- mixer_output: bfloat16 [65536, 2560], P(('dp', 'ctx')), parts along dimension 0
- attention_output: bfloat16 [65536, 2560], P(('dp', 'ctx')), parts along dimension 0
The draws below stay inside these ranges and needn't reach their ends.
There are 16 independent parts, one for each index of `dp`. The reference program is written for one: setup_inputs(seed, part) draws one part's arguments, and reference() takes and returns one part's arrays. A program takes and returns all parts, laid end to end along the dimension named above; each array names one. Nothing has to cross between parts.
All inputs are finite; a program needn't handle non-finite values.
Results may differ from the reference program's by a relative error of at most 0.0049.
Values may be sent and summed in bfloat16 or wider, within the bound.
No kernel may reach another device: no remote copies, remote signals or barrier semaphores. Data moves between devices by JAX's collectives and lax.ppermute only.
A program may use at most 128 MiB of HBM per device.

```python
import math
import jax
import jax.numpy as jnp
from jax import lax

MIXER_HEADS = 40
P_SIZE = 64
N = 128
QH = 32
KVH = 4
DH = 80
STRETCH = 128
TOK_DEV = 128
SEQUENCE_LENGTH = 4096


def draw_query_rows(key, part):
    base = jax.random.fold_in(key, 1)
    values = jnp.clip(jax.random.normal(base, (SEQUENCE_LENGTH, QH * DH), jnp.float32), -6.0, 6.0)
    return values.astype(jnp.bfloat16)


def draw_key_rows(key, part):
    base = jax.random.fold_in(key, 2)
    values = jnp.clip(jax.random.normal(base, (SEQUENCE_LENGTH, KVH * DH), jnp.float32), -6.0, 6.0)
    return values.astype(jnp.bfloat16)


def draw_log_decay(key, part):
    random_keys = jax.random.split(jax.random.fold_in(key, 5), 7)
    slow_share = 0.6
    picked = jax.random.uniform(random_keys[0], (MIXER_HEADS,), jnp.float32) < slow_share
    slow_rate = jnp.exp(jax.random.uniform(random_keys[1], (MIXER_HEADS,), jnp.float32, math.log(0.1 / SEQUENCE_LENGTH), math.log(0.5 / SEQUENCE_LENGTH)))
    fast_rate = jnp.exp(jax.random.uniform(random_keys[2], (MIXER_HEADS,), jnp.float32, math.log(0.5 / SEQUENCE_LENGTH), math.log(0.04)))
    event_rate = jnp.where(picked, slow_rate, fast_rate)
    device_multiplier = jax.random.uniform(random_keys[3], (SEQUENCE_LENGTH // TOK_DEV, 1, MIXER_HEADS), jnp.float32, 0.5, 1.5)
    device_multiplier = jnp.broadcast_to(device_multiplier, (SEQUENCE_LENGTH // TOK_DEV, TOK_DEV, MIXER_HEADS)).reshape(SEQUENCE_LENGTH, MIXER_HEADS)
    coarse_estimate = jax.random.uniform(random_keys[4], (SEQUENCE_LENGTH, MIXER_HEADS), jnp.float32, 0.5, 1.5)
    third_portion = SEQUENCE_LENGTH // 3
    spurt_location = jnp.arange(3, dtype=jnp.int32) * third_portion + jax.random.randint(random_keys[5], (3,), 0, third_portion)
    spurt_retain = jnp.log(jax.random.uniform(random_keys[6], (3, MIXER_HEADS), jnp.float32, 0.5, 0.8))
    match_count = (jnp.arange(SEQUENCE_LENGTH, dtype=jnp.int32)[:, None] == spurt_location[None, :]).astype(jnp.float32)
    spurt_list = jnp.sum(match_count[:, :, None] * spurt_retain[None], axis=1)
    return -event_rate[None, :] * device_multiplier * coarse_estimate + spurt_list


def shard_levels(own_key, dims, pieces, least, top_value):
    def one(dim, blocks):
        heights = jax.random.uniform(jax.random.fold_in(jax.random.fold_in(own_key, 6), dim), (blocks,), jnp.float32, least / len(pieces), top_value / len(pieces))
        return jnp.repeat(jnp.exp(heights), dims[dim] // blocks).reshape((-1,) + (1,) * (len(dims) - dim - 1))

    factor_of = one(*pieces[0])
    for cut in pieces[1:]:
        factor_of = factor_of * one(*cut)
    return factor_of


def scatter_about(rng, shape, spread, reach, shards=(), kind=jnp.bfloat16):
    entries = jax.random.normal(rng, shape, jnp.float32) * spread
    if len(shards) > 0:
        entries = shard_levels(rng, shape, shards, -0.22, 0.18) * entries
    return jnp.clip(entries, min=-reach, max=reach).astype(kind)


def setup_inputs(seed: int = 0, part: int = 0) -> dict:
    splits = jax.random.split(jax.random.key(seed), 8)
    own_keys = jax.random.split(jax.random.fold_in(splits[7], part), 8)
    mixer_input = scatter_about(own_keys[0], (SEQUENCE_LENGTH, MIXER_HEADS * P_SIZE), 1.0, 6.0, ((0, 32),))
    input_map = scatter_about(own_keys[1], (SEQUENCE_LENGTH, N), 1.0, 6.0, ((0, 32),))
    output_map = scatter_about(own_keys[2], (SEQUENCE_LENGTH, N), (N * SEQUENCE_LENGTH // 4) ** -0.5, 0.015625, ((0, 32),))
    log_decay = draw_log_decay(jax.random.fold_in(jax.random.fold_in(splits[7], part), 71), part)
    query_rows = draw_query_rows(jax.random.fold_in(jax.random.fold_in(splits[7], part), 71), part)
    key_rows = draw_key_rows(jax.random.fold_in(jax.random.fold_in(splits[7], part), 71), part)
    value_rows = scatter_about(own_keys[6], (SEQUENCE_LENGTH, KVH * DH), 1.0, 6.0, ((0, 32),))
    return dict(mixer_input=mixer_input, input_map=input_map, output_map=output_map, log_decay=log_decay, query_rows=query_rows, key_rows=key_rows, value_rows=value_rows)


masked_score = -1e+30

def mixer_part(mixer_input, input_map, output_map, log_decay):
    length = mixer_input.shape[0]
    count = length // STRETCH
    x_blocks = mixer_input.reshape(count, STRETCH, MIXER_HEADS, P_SIZE)
    in_blocks = input_map.reshape(count, STRETCH, N)
    out_blocks = output_map.reshape(count, STRETCH, N)
    decay_blocks = log_decay.reshape(count, STRETCH, MIXER_HEADS)
    lower_mask = jnp.tril(jnp.ones((STRETCH, STRETCH), dtype=bool))

    def advance(state, items):
        x_block, in_block, out_block, decay_block = items
        cumulative = jnp.cumsum(decay_block, axis=0).T
        match = jnp.dot(out_block, in_block.T, preferred_element_type=jnp.float32)
        decay_gap = jnp.where(lower_mask[None], cumulative[:, :, None] - cumulative[:, None, :], 0.0)
        weights = jnp.where(lower_mask[None], match[None] * jnp.exp(decay_gap), 0.0).astype(jnp.bfloat16)
        inner = jnp.einsum('hts,shp->thp', weights.astype(jnp.float32), x_block.astype(jnp.float32))
        carried = jnp.einsum('tn,hnp->thp', out_block.astype(jnp.float32), state, precision=lax.Precision.HIGHEST)
        carried = carried * jnp.exp(cumulative).T[:, :, None]
        result = (inner + carried).astype(jnp.bfloat16)
        weighted = (jnp.exp(cumulative[:, -1:] - cumulative)[:, :, None] * in_block.astype(jnp.float32)[None]).astype(jnp.bfloat16)
        update = jnp.einsum('hsn,shp->hnp', weighted.astype(jnp.float32), x_block.astype(jnp.float32))
        state = jnp.exp(cumulative[:, -1])[:, None, None] * state + update
        return (state, result)
    start_state = jnp.zeros((MIXER_HEADS, N, P_SIZE), jnp.float32)
    unused, results = lax.scan(advance, start_state, (x_blocks, in_blocks, out_blocks, decay_blocks))
    return results.reshape(length, MIXER_HEADS * P_SIZE)

def attention_part(query_rows, key_rows, value_rows):
    length = query_rows.shape[0]
    group = QH // KVH
    scale = 1.0 / math.sqrt(DH)
    causal = jnp.tril(jnp.ones((length, length), dtype=bool))

    def one_head(head):
        kv_head = head // group
        query_cols = lax.dynamic_slice_in_dim(query_rows, (head * DH).astype(jnp.int32), DH, 1)
        key_cols = lax.dynamic_slice_in_dim(key_rows, (kv_head * DH).astype(jnp.int32), DH, 1)
        value_cols = lax.dynamic_slice_in_dim(value_rows, (kv_head * DH).astype(jnp.int32), DH, 1)
        scores = jnp.dot(query_cols, key_cols.T, preferred_element_type=jnp.float32) * scale
        scores = jnp.where(causal, scores, masked_score)
        top = lax.optimization_barrier(jnp.max(scores, axis=-1, keepdims=True))
        expo = jnp.exp(scores - top)
        total = lax.optimization_barrier(jnp.sum(expo, axis=-1, keepdims=True))
        summed = jnp.dot(expo.astype(jnp.bfloat16), value_cols, preferred_element_type=jnp.float32)
        return (summed / total).astype(jnp.bfloat16)
    outputs = lax.map(one_head, jnp.arange(QH, dtype=jnp.int32))
    return outputs.transpose(1, 0, 2).reshape(length, QH * DH)

def reference(mixer_input, input_map, output_map, log_decay, query_rows, key_rows, value_rows):
    mixer_output = mixer_part(mixer_input, input_map, output_map, log_decay)
    attention_output = attention_part(query_rows, key_rows, value_rows)
    return (mixer_output, attention_output)
```

```python
import math

import jax
import jax.numpy as jnp
from jax import lax
from jax.experimental import pallas as pl
from jax.experimental.pallas import tpu as pltpu
from jax.sharding import Mesh
from jax.sharding import PartitionSpec as P

MIXER_HEADS = 40
P_SIZE = 64
N = 128
QH = 32
KVH = 4
DH = 80
T = 128
WIDTH = MIXER_HEADS * P_SIZE
GROUP = QH // KVH
GDH = GROUP * DH
NX = 4
NZ = 8
NCTX = NX * NZ
PIECE_ROWS = 16
PIECE_COLS = 640
masked_score = -1e30
F32 = jnp.float32
BF16 = jnp.bfloat16


def split2(a):
    hi = a.astype(BF16)
    return hi, (a - hi.astype(F32)).astype(BF16)


def dot(a, b):
    return jnp.dot(a, b, preferred_element_type=F32)


def dot_nt(a, b):
    return lax.dot_general(a, b, (((1,), (1,)), ((), ())), preferred_element_type=F32)


def head_spread():
    rows = lax.broadcasted_iota(jnp.int32, (MIXER_HEADS, WIDTH), 0)
    cols = lax.broadcasted_iota(jnp.int32, (MIXER_HEADS, WIDTH), 1)
    return jnp.where(cols // P_SIZE == rows, 1.0, 0.0).astype(BF16)


def spread(a, onehot):
    hi, lo = split2(a)
    return dot(hi, onehot) + dot(lo, onehot)


def cumulative_of(decay):
    rows = lax.broadcasted_iota(jnp.int32, (T, T), 0)
    cols = lax.broadcasted_iota(jnp.int32, (T, T), 1)
    lower = jnp.where(cols <= rows, 1.0, 0.0).astype(F32)
    return jnp.dot(lower, decay, precision=lax.Precision.HIGHEST, preferred_element_type=F32)


def update_kernel(x_ref, in_ref, decay_ref, out_ref):
    cumulative = cumulative_of(decay_ref[...])
    last = cumulative[T - 1 : T, :]
    onehot = head_spread()
    tail = spread(jnp.exp(last - cumulative), onehot)
    hi, lo = split2(x_ref[...].astype(F32) * tail)
    in_t = in_ref[...].astype(F32).T.astype(BF16)
    update = (dot(in_t, hi) + dot(in_t, lo)).astype(BF16)
    total = jnp.broadcast_to(jnp.exp(last), (PIECE_ROWS, MIXER_HEADS))
    total_hi, total_lo = split2(total)
    head = lax.broadcasted_iota(jnp.int32, (MIXER_HEADS, 128), 0)
    lane = lax.broadcasted_iota(jnp.int32, (MIXER_HEADS, 128), 1)
    place_hi = jnp.where(lane == head, 1.0, 0.0).astype(BF16)
    place_lo = jnp.where(lane == head + 64, 1.0, 0.0).astype(BF16)
    factor = (dot(total_hi, place_hi) + dot(total_lo, place_lo)).astype(BF16)
    for i in range(N // PIECE_ROWS):
        for j in range(WIDTH // PIECE_COLS):
            d = i * (WIDTH // PIECE_COLS) + j
            out_ref[d, :, :PIECE_COLS] = update[
                i * PIECE_ROWS : (i + 1) * PIECE_ROWS, j * PIECE_COLS : (j + 1) * PIECE_COLS
            ]
            out_ref[d, :, PIECE_COLS:] = factor


def prefix_kernel(place_ref, in_ref, out_ref):
    first_head = (place_ref[0] % (WIDTH // PIECE_COLS)) * (PIECE_COLS // P_SIZE)
    lane = lax.broadcasted_iota(jnp.int32, (128, PIECE_COLS), 0)
    cols = lax.broadcasted_iota(jnp.int32, (128, PIECE_COLS), 1)
    head = first_head + cols // P_SIZE
    onehot = jnp.where((lane == head) | (lane == head + 64), 1.0, 0.0).astype(BF16)
    state = jnp.zeros((PIECE_ROWS, PIECE_COLS), F32)
    for k in range(NCTX):
        out_ref[k] = state.astype(BF16)
        factor = dot(in_ref[k, :, PIECE_COLS:], onehot)
        state = factor * state + in_ref[k, :, :PIECE_COLS].astype(F32)


def mix_kernel(x_ref, in_ref, map_ref, decay_ref, enter_ref, out_ref):
    cumulative = cumulative_of(decay_ref[...])
    middle = 0.5 * cumulative[T - 1 : T, :]
    onehot = head_spread()
    ahead = spread(jnp.exp(cumulative - middle), onehot)
    behind = spread(jnp.exp(middle - cumulative), onehot)
    start = spread(jnp.exp(jnp.broadcast_to(middle, (8, MIXER_HEADS))), onehot)[0:1, :]
    hi, lo = split2(x_ref[...].astype(F32) * behind)
    out_map = map_ref[...]
    match = dot_nt(out_map, in_ref[...])
    rows = lax.broadcasted_iota(jnp.int32, (T, T), 0)
    cols = lax.broadcasted_iota(jnp.int32, (T, T), 1)
    match_hi, match_lo = split2(jnp.where(cols <= rows, match, 0.0))
    inner = dot(match_hi, hi) + dot(match_hi, lo) + dot(match_lo, hi)
    for j in range(WIDTH // PIECE_COLS):
        cut = slice(j * PIECE_COLS, (j + 1) * PIECE_COLS)
        entering = jnp.concatenate(
            [enter_ref[i * (WIDTH // PIECE_COLS) + j] for i in range(N // PIECE_ROWS)], axis=0
        )
        carried = dot(out_map, entering)
        out_ref[:, cut] = (ahead[:, cut] * (inner[:, cut] + start[:, cut] * carried)).astype(BF16)


QT = 256
CHUNK = NZ * T


def attend_kernel(place_ref, q_ref, kv_ref, out_ref, k_buf, v_buf, q_buf, o_buf):
    z = place_ref[0]
    pad = jnp.zeros((128 - DH, CHUNK), BF16)
    ones = jnp.where(lax.broadcasted_iota(jnp.int32, (16, CHUNK), 0) == 0, 1.0, 0.0).astype(BF16)
    for c in range(NX):
        cut = slice(c * CHUNK, (c + 1) * CHUNK)
        k_buf[DH:128, cut] = pad
        k_buf[128 + DH : 256, cut] = pad
        v_buf[DH : DH + 16, cut] = ones
        for b in range(NZ):
            at = slice(c * CHUNK + b * T, c * CHUNK + (b + 1) * T)
            k = kv_ref[b, c, :DH, :]
            k_buf[:DH, at] = k
            k_buf[128 : 128 + DH, at] = k
            v_buf[:DH, at] = kv_ref[b, c, DH:, :]
    scale = math.log2(math.e) / math.sqrt(DH)
    zero = jnp.zeros((T, 128 - DH), F32)
    for c in range(NX):
        for h in range(GROUP):
            q = q_ref[c, :, h * DH : (h + 1) * DH].astype(F32) * scale
            hi, lo = split2(jnp.concatenate([q, zero], axis=1))
            q_buf[c, h * T : (h + 1) * T, :128] = hi
            q_buf[c, h * T : (h + 1) * T, 128:] = lo
    row = lax.broadcasted_iota(jnp.int32, (QT, CHUNK), 0) % T
    col = lax.broadcasted_iota(jnp.int32, (QT, CHUNK), 1)
    visible = col <= row + z * T
    for c in range(NX):
        seen = c * CHUNK

        def one_tile(i, carry, c=c, seen=seen):
            at = pl.ds(pl.multiple_of(i * QT, QT), QT)
            q = q_buf[c, at, :]
            near = dot(q, k_buf[:, seen : seen + CHUNK])
            near = jnp.where(visible, near, masked_score)
            top = jnp.max(near, axis=1, keepdims=True)
            if c:
                far = dot(q, k_buf[:, :seen])
                top = jnp.maximum(top, jnp.max(far, axis=1, keepdims=True))
            total = dot_nt(jnp.exp2(near - top).astype(BF16), v_buf[:, seen : seen + CHUNK])
            if c:
                total += dot_nt(jnp.exp2(far - top).astype(BF16), v_buf[:, :seen])
            o_buf[at, :] = total[:, :DH] / total[:, DH : DH + 1]
            return carry

        lax.fori_loop(0, GROUP * T // QT, one_tile, 0)
        out_ref[c] = jnp.concatenate(
            [o_buf[h * T : (h + 1) * T, :] for h in range(GROUP)], axis=1
        ).astype(BF16)


VMEM_SPEC = pl.BlockSpec(memory_space=pltpu.VMEM)
SMEM_SPEC = pl.BlockSpec(memory_space=pltpu.SMEM)


def call(kernel, shape, specs, scratch=(), limit=48):
    return pl.pallas_call(
        kernel,
        out_shape=jax.ShapeDtypeStruct(shape, BF16),
        in_specs=specs,
        out_specs=VMEM_SPEC,
        scratch_shapes=list(scratch),
        compiler_params=pltpu.CompilerParams(vmem_limit_bytes=limit << 20),
    )


def per_device(mixer_input, input_map, output_map, log_decay, query_rows, key_rows, value_rows):
    place_z = lax.axis_index("cz").astype(jnp.int32).reshape(1)
    place = (lax.axis_index("cx") * NZ + lax.axis_index("cz")).astype(jnp.int32).reshape(1)
    kv = jnp.concatenate(
        [key_rows.T.reshape(KVH, DH, T), value_rows.T.reshape(KVH, DH, T)], axis=1
    )
    kv = lax.all_to_all(kv, "cx", 0, 0)
    kv = lax.all_gather(kv, "cz")
    q = query_rows.reshape(T, KVH, GDH).transpose(1, 0, 2)
    q = lax.all_to_all(q, "cx", 0, 0)
    update = call(
        update_kernel, (NCTX, PIECE_ROWS, PIECE_COLS + 128), [VMEM_SPEC] * 3
    )(mixer_input, input_map, log_decay)
    update = lax.all_to_all(update, ("cx", "cz"), 0, 0)
    entering = call(prefix_kernel, (NCTX, PIECE_ROWS, PIECE_COLS), [SMEM_SPEC, VMEM_SPEC])(
        place, update
    )
    entering = lax.all_to_all(entering, ("cx", "cz"), 0, 0)
    attended = call(
        attend_kernel,
        (NX, T, GDH),
        [SMEM_SPEC, VMEM_SPEC, VMEM_SPEC],
        [
            pltpu.VMEM((256, NX * CHUNK), BF16),
            pltpu.VMEM((DH + 16, NX * CHUNK), BF16),
            pltpu.VMEM((NX, GROUP * T, 256), BF16),
            pltpu.VMEM((GROUP * T, DH), F32),
        ],
    )(place_z, q, kv)
    attended = lax.all_to_all(attended, "cx", 0, 0)
    attention_output = attended.transpose(1, 0, 2).reshape(T, QH * DH)
    mixer_output = call(mix_kernel, (T, WIDTH), [VMEM_SPEC] * 5)(
        mixer_input, input_map, output_map, log_decay, entering
    )
    return mixer_output, attention_output


def solution(mesh):
    grid = Mesh(mesh.devices.reshape(-1, NX, NZ), ("dp", "cx", "cz"))
    spec = P(("dp", "cx", "cz"), None)
    return jax.shard_map(
        per_device,
        mesh=grid,
        in_specs=(spec,) * 7,
        out_specs=(spec, spec),
        check_vma=False,
    )
```

```python
import math

import jax
import jax.numpy as jnp
from jax import lax
from jax.experimental import pallas as pl
from jax.experimental.pallas import tpu as pltpu
from jax.sharding import Mesh
from jax.sharding import PartitionSpec as P

MIXER_HEADS = 40
P_SIZE = 64
N = 128
QH = 32
KVH = 4
DH = 80
T = 128
WIDTH = MIXER_HEADS * P_SIZE
GROUP = QH // KVH
GDH = GROUP * DH
NX = 4
NZ = 8
NCTX = NX * NZ
PIECE_ROWS = 16
PIECE_COLS = 640
masked_score = -1e30
F32 = jnp.float32
BF16 = jnp.bfloat16


def split2(a):
    hi = a.astype(BF16)
    return hi, (a - hi.astype(F32)).astype(BF16)


def dot(a, b):
    return jnp.dot(a, b, preferred_element_type=F32)


def dot_nt(a, b):
    return lax.dot_general(a, b, (((1,), (1,)), ((), ())), preferred_element_type=F32)


def head_spread():
    rows = lax.broadcasted_iota(jnp.int32, (MIXER_HEADS, WIDTH), 0)
    cols = lax.broadcasted_iota(jnp.int32, (MIXER_HEADS, WIDTH), 1)
    return jnp.where(cols // P_SIZE == rows, 1.0, 0.0).astype(BF16)


def spread(a, onehot):
    hi, lo = split2(a)
    return dot(hi, onehot) + dot(lo, onehot)


def cumulative_of(decay):
    rows = lax.broadcasted_iota(jnp.int32, (T, T), 0)
    cols = lax.broadcasted_iota(jnp.int32, (T, T), 1)
    lower = jnp.where(cols <= rows, 1.0, 0.0).astype(F32)
    return jnp.dot(lower, decay, precision=lax.Precision.HIGHEST, preferred_element_type=F32)


def update_kernel(x_ref, in_ref, decay_ref, after_ref, out_ref):
    cumulative = cumulative_of(decay_ref[...])
    last = cumulative[T - 1 : T, :]
    onehot = head_spread()
    tail = spread(jnp.exp(last - cumulative), onehot)
    hi, lo = split2(x_ref[...].astype(F32) * tail)
    in_t = in_ref[...].astype(F32).T.astype(BF16)
    update = (dot(in_t, hi) + dot(in_t, lo)).astype(BF16)
    total = jnp.broadcast_to(jnp.exp(last), (PIECE_ROWS, MIXER_HEADS))
    total_hi, total_lo = split2(total)
    head = lax.broadcasted_iota(jnp.int32, (MIXER_HEADS, 128), 0)
    lane = lax.broadcasted_iota(jnp.int32, (MIXER_HEADS, 128), 1)
    place_hi = jnp.where(lane == head, 1.0, 0.0).astype(BF16)
    place_lo = jnp.where(lane == head + 64, 1.0, 0.0).astype(BF16)
    factor = (dot(total_hi, place_hi) + dot(total_lo, place_lo)).astype(BF16)
    for i in range(N // PIECE_ROWS):
        for j in range(WIDTH // PIECE_COLS):
            d = i * (WIDTH // PIECE_COLS) + j
            out_ref[d, :, :PIECE_COLS] = update[
                i * PIECE_ROWS : (i + 1) * PIECE_ROWS, j * PIECE_COLS : (j + 1) * PIECE_COLS
            ]
            out_ref[d, :, PIECE_COLS:] = factor


def prefix_kernel(place_ref, in_ref, out_ref):
    first_head = (place_ref[0] % (WIDTH // PIECE_COLS)) * (PIECE_COLS // P_SIZE)
    lane = lax.broadcasted_iota(jnp.int32, (128, PIECE_COLS), 0)
    cols = lax.broadcasted_iota(jnp.int32, (128, PIECE_COLS), 1)
    head = first_head + cols // P_SIZE
    onehot = jnp.where((lane == head) | (lane == head + 64), 1.0, 0.0).astype(BF16)
    state = jnp.zeros((PIECE_ROWS, PIECE_COLS), F32)
    for k in range(NCTX):
        out_ref[k] = state.astype(BF16)
        factor = dot(in_ref[k, :, PIECE_COLS:], onehot)
        state = factor * state + in_ref[k, :, :PIECE_COLS].astype(F32)


def mix_kernel(x_ref, in_ref, map_ref, decay_ref, enter_ref, out_ref):
    cumulative = cumulative_of(decay_ref[...])
    middle = 0.5 * cumulative[T - 1 : T, :]
    onehot = head_spread()
    ahead = spread(jnp.exp(cumulative - middle), onehot)
    behind = spread(jnp.exp(middle - cumulative), onehot)
    start = spread(jnp.exp(jnp.broadcast_to(middle, (8, MIXER_HEADS))), onehot)[0:1, :]
    hi, lo = split2(x_ref[...].astype(F32) * behind)
    out_map = map_ref[...]
    match = dot_nt(out_map, in_ref[...])
    rows = lax.broadcasted_iota(jnp.int32, (T, T), 0)
    cols = lax.broadcasted_iota(jnp.int32, (T, T), 1)
    match_hi, match_lo = split2(jnp.where(cols <= rows, match, 0.0))
    inner = dot(match_hi, hi) + dot(match_hi, lo) + dot(match_lo, hi)
    for j in range(WIDTH // PIECE_COLS):
        cut = slice(j * PIECE_COLS, (j + 1) * PIECE_COLS)
        entering = jnp.concatenate(
            [enter_ref[i * (WIDTH // PIECE_COLS) + j] for i in range(N // PIECE_ROWS)], axis=0
        )
        carried = dot(out_map, entering)
        out_ref[:, cut] = (ahead[:, cut] * (inner[:, cut] + start[:, cut] * carried)).astype(BF16)


CHUNK = NZ * T
QUERIES = GROUP * T
KEYS = 512


def pack_kernel(q_ref, k_ref, v_ref, out_ref):
    pad = jnp.zeros((T, 384 - KVH * DH), F32)
    k = jnp.concatenate([k_ref[...].astype(F32), pad], axis=1).T.astype(BF16)
    v = jnp.concatenate([v_ref[...].astype(F32), pad], axis=1).T.astype(BF16)
    for g in range(KVH):
        q = q_ref[:, g * GDH : (g + 1) * GDH].astype(F32)
        out_ref[g, :GDH, :] = q.T.astype(BF16)
        out_ref[g, GDH : GDH + DH, :] = k[g * DH : (g + 1) * DH, :]
        out_ref[g, GDH + DH :, :] = v[g * DH : (g + 1) * DH, :]


def attend_kernel(place_ref, q_ref, kv_ref, after_ref, out_ref, kv_buf, k_buf, v_buf, q_buf, sems):
    copies = [
        pltpu.make_async_copy(kv_ref.at[:, c], kv_buf.at[c], sems.at[c]) for c in range(NX)
    ]
    for copy in copies:
        copy.start()
    z = place_ref[0]
    scale = math.log2(math.e) / math.sqrt(DH)
    row = lax.broadcasted_iota(jnp.int32, (KEYS, QUERIES), 0)
    col = lax.broadcasted_iota(jnp.int32, (KEYS, QUERIES), 1) % T
    ones = jnp.where(lax.broadcasted_iota(jnp.int32, (16, CHUNK), 0) == 0, 1.0, 0.0).astype(BF16)
    blank = jnp.zeros((128 - DH, T), F32)
    blank_q = jnp.zeros((128 - DH, QUERIES), BF16)
    for c in range(NX):
        q_buf[DH:128, :] = blank_q
        q_buf[128 + DH :, :] = blank_q
        for h in range(GROUP):
            hi, lo = split2(q_ref[c, h * DH : (h + 1) * DH, :].astype(F32) * scale)
            q_buf[:DH, h * T : (h + 1) * T] = hi
            q_buf[128 : 128 + DH, h * T : (h + 1) * T] = lo
        copies[c].wait()
        v_buf[DH:, c * CHUNK : (c + 1) * CHUNK] = ones
        for b in range(NZ):
            at = slice(c * CHUNK + b * T, c * CHUNK + (b + 1) * T)
            v_buf[:DH, at] = kv_buf[c, b, DH:, :]
            k = jnp.concatenate([kv_buf[c, b, :DH, :].astype(F32), blank], axis=0).T.astype(BF16)
            k_buf[at, :128] = k
            k_buf[at, 128:] = k
        q = q_buf[...]

        def scores(j, c=c, q=q):
            found = dot(k_buf[j * KEYS : (j + 1) * KEYS, :], q)
            if j * KEYS >= c * CHUNK:
                seen = row + (j * KEYS - c * CHUNK) <= col + z * T
                found = jnp.where(seen, found, masked_score)
            return found

        count = (c + 1) * CHUNK // KEYS
        found = scores(0)
        top = jnp.max(found, axis=0, keepdims=True)
        total = None
        for j in range(count):
            later = scores(j + 1) if j + 1 < count else None
            expos = jnp.exp2(found - top).astype(BF16)
            summed = dot(v_buf[:, j * KEYS : (j + 1) * KEYS], expos)
            total = summed if total is None else total + summed
            if later is not None:
                raised = jnp.maximum(top, jnp.max(later, axis=0, keepdims=True))
                total = total * jnp.exp2(top - raised)
                top = raised
                found = later
        done = (total[:DH, :] / total[DH : DH + 1, :]).astype(BF16)
        for h in range(GROUP):
            out_ref[c, h * DH : (h + 1) * DH, :] = done[:, h * T : (h + 1) * T]


def place_kernel(in_ref, after_ref, out_ref):
    for g in range(KVH):
        out_ref[:, g * GDH : (g + 1) * GDH] = in_ref[g].astype(F32).T.astype(BF16)


VMEM_SPEC = pl.BlockSpec(memory_space=pltpu.VMEM)
SMEM_SPEC = pl.BlockSpec(memory_space=pltpu.SMEM)
ANY_SPEC = pl.BlockSpec(memory_space=pl.ANY)


def call(kernel, shape, specs, scratch=(), limit=48):
    return pl.pallas_call(
        kernel,
        out_shape=jax.ShapeDtypeStruct(shape, BF16),
        in_specs=specs,
        out_specs=VMEM_SPEC,
        scratch_shapes=list(scratch),
        compiler_params=pltpu.CompilerParams(vmem_limit_bytes=limit << 20),
    )


def per_device(mixer_input, input_map, output_map, log_decay, query_rows, key_rows, value_rows):
    place_z = lax.axis_index("cz").astype(jnp.int32).reshape(1)
    place = (lax.axis_index("cx") * NZ + lax.axis_index("cz")).astype(jnp.int32).reshape(1)
    packed = call(pack_kernel, (KVH, GDH + 2 * DH, T), [VMEM_SPEC] * 3)(
        query_rows, key_rows, value_rows
    )
    packed = lax.all_to_all(packed, "cx", 0, 0)
    kv_part = packed[:, GDH:, :]
    kv = lax.all_gather(kv_part, "cz")
    update = call(
        update_kernel, (NCTX, PIECE_ROWS, PIECE_COLS + 128), [VMEM_SPEC] * 3 + [ANY_SPEC]
    )(mixer_input, input_map, log_decay, packed)
    update = lax.all_to_all(update, ("cx", "cz"), 0, 0)
    prefix = call(prefix_kernel, (NCTX, PIECE_ROWS, PIECE_COLS), [SMEM_SPEC, VMEM_SPEC])(
        place, update
    )
    entering = lax.all_to_all(prefix, ("cx", "cz"), 0, 0)
    attended = call(
        attend_kernel,
        (NX, GDH, T),
        [SMEM_SPEC, VMEM_SPEC, ANY_SPEC, ANY_SPEC],
        [
            pltpu.VMEM((NX, NZ, 2 * DH, T), BF16),
            pltpu.VMEM((NX * CHUNK, 256), BF16),
            pltpu.VMEM((DH + 16, NX * CHUNK), BF16),
            pltpu.VMEM((256, QUERIES), BF16),
            pltpu.SemaphoreType.DMA((NX,)),
        ],
    )(place_z, packed, kv, prefix)
    attended = lax.all_to_all(attended, "cx", 0, 0)
    mixer_output = call(mix_kernel, (T, WIDTH), [VMEM_SPEC] * 5)(
        mixer_input, input_map, output_map, log_decay, entering
    )
    attention_output = call(place_kernel, (T, QH * DH), [VMEM_SPEC, VMEM_SPEC])(
        attended, mixer_output[:16, :128]
    )
    return mixer_output, attention_output


def solution(mesh):
    grid = Mesh(mesh.devices.reshape(-1, NX, NZ), ("dp", "cx", "cz"))
    spec = P(("dp", "cx", "cz"), None)
    return jax.shard_map(
        per_device,
        mesh=grid,
        in_specs=(spec,) * 7,
        out_specs=(spec, spec),
        check_vma=False,
    )
```

```python
import math

import jax
import jax.numpy as jnp
from jax import lax
from jax.experimental import pallas as pl
from jax.experimental.pallas import tpu as pltpu
from jax.sharding import Mesh
from jax.sharding import PartitionSpec as P

MIXER_HEADS = 40
P_SIZE = 64
N = 128
QH = 32
KVH = 4
DH = 80
T = 128
WIDTH = MIXER_HEADS * P_SIZE
GROUP = QH // KVH
GDH = GROUP * DH
NX = 4
NH = 4
NZ = 2 * NH
NCTX = NX * NZ
PIECE_ROWS = 16
PIECE_COLS = 640
masked_score = -1e30
F32 = jnp.float32
BF16 = jnp.bfloat16


def split2(a):
    hi = a.astype(BF16)
    return hi, (a - hi.astype(F32)).astype(BF16)


def dot(a, b):
    return jnp.dot(a, b, preferred_element_type=F32)


def dot_nt(a, b):
    return lax.dot_general(a, b, (((1,), (1,)), ((), ())), preferred_element_type=F32)


def head_spread():
    rows = lax.broadcasted_iota(jnp.int32, (MIXER_HEADS, WIDTH), 0)
    cols = lax.broadcasted_iota(jnp.int32, (MIXER_HEADS, WIDTH), 1)
    return jnp.where(cols // P_SIZE == rows, 1.0, 0.0).astype(BF16)


def spread(a, onehot):
    hi, lo = split2(a)
    return dot(hi, onehot) + dot(lo, onehot)


def cumulative_of(decay):
    rows = lax.broadcasted_iota(jnp.int32, (T, T), 0)
    cols = lax.broadcasted_iota(jnp.int32, (T, T), 1)
    lower = jnp.where(cols <= rows, 1.0, 0.0).astype(F32)
    return lax.dot_general(
        lower,
        decay,
        (((1,), (1,)), ((), ())),
        precision=lax.Precision.HIGHEST,
        preferred_element_type=F32,
    )


def update_kernel(x_ref, in_ref, decay_ref, out_ref):
    cumulative = cumulative_of(decay_ref[...])
    last = cumulative[T - 1 : T, :]
    onehot = head_spread()
    tail = spread(jnp.exp(last - cumulative), onehot)
    hi, lo = split2(x_ref[...].astype(F32) * tail)
    in_t = in_ref[...].astype(F32).T.astype(BF16)
    update = (dot(in_t, hi) + dot(in_t, lo)).astype(BF16)
    total = jnp.broadcast_to(jnp.exp(last), (PIECE_ROWS, MIXER_HEADS))
    total_hi, total_lo = split2(total)
    head = lax.broadcasted_iota(jnp.int32, (MIXER_HEADS, 128), 0)
    lane = lax.broadcasted_iota(jnp.int32, (MIXER_HEADS, 128), 1)
    place_hi = jnp.where(lane == head, 1.0, 0.0).astype(BF16)
    place_lo = jnp.where(lane == head + 64, 1.0, 0.0).astype(BF16)
    factor = (dot(total_hi, place_hi) + dot(total_lo, place_lo)).astype(BF16)
    for i in range(N // PIECE_ROWS):
        for j in range(WIDTH // PIECE_COLS):
            d = i * (WIDTH // PIECE_COLS) + j
            out_ref[d, :, :PIECE_COLS] = update[
                i * PIECE_ROWS : (i + 1) * PIECE_ROWS, j * PIECE_COLS : (j + 1) * PIECE_COLS
            ]
            out_ref[d, :, PIECE_COLS:] = factor


def prefix_kernel(place_ref, in_ref, after_ref, out_ref):
    first_head = (place_ref[0] % (WIDTH // PIECE_COLS)) * (PIECE_COLS // P_SIZE)
    lane = lax.broadcasted_iota(jnp.int32, (128, PIECE_COLS), 0)
    cols = lax.broadcasted_iota(jnp.int32, (128, PIECE_COLS), 1)
    head = first_head + cols // P_SIZE
    onehot = jnp.where((lane == head) | (lane == head + 64), 1.0, 0.0).astype(BF16)
    state = jnp.zeros((PIECE_ROWS, PIECE_COLS), F32)
    for k in range(NCTX):
        out_ref[k] = state.astype(BF16)
        factor = dot(in_ref[k, :, PIECE_COLS:], onehot)
        state = factor * state + in_ref[k, :, :PIECE_COLS].astype(F32)


def mix_kernel(x_ref, in_ref, map_ref, decay_ref, enter_ref, out_ref):
    cumulative = cumulative_of(decay_ref[...])
    middle = 0.5 * cumulative[T - 1 : T, :]
    onehot = head_spread()
    ahead = spread(jnp.exp(cumulative - middle), onehot)
    behind = spread(jnp.exp(middle - cumulative), onehot)
    start = spread(jnp.exp(jnp.broadcast_to(middle, (8, MIXER_HEADS))), onehot)[0:1, :]
    hi, lo = split2(x_ref[...].astype(F32) * behind)
    out_map = map_ref[...]
    match = dot_nt(out_map, in_ref[...])
    rows = lax.broadcasted_iota(jnp.int32, (T, T), 0)
    cols = lax.broadcasted_iota(jnp.int32, (T, T), 1)
    match_hi, match_lo = split2(jnp.where(cols <= rows, match, 0.0))
    inner = dot(match_hi, hi) + dot(match_hi, lo) + dot(match_lo, hi)
    for j in range(WIDTH // PIECE_COLS):
        cut = slice(j * PIECE_COLS, (j + 1) * PIECE_COLS)
        entering = jnp.concatenate(
            [enter_ref[i * (WIDTH // PIECE_COLS) + j] for i in range(N // PIECE_ROWS)], axis=0
        )
        carried = dot(out_map, entering)
        out_ref[:, cut] = (ahead[:, cut] * (inner[:, cut] + start[:, cut] * carried)).astype(BF16)


CHUNK = NZ * T
QUERIES = GROUP * T
KEYS = 512


def pack_kernel(q_ref, k_ref, v_ref, out_ref):
    for g in range(KVH):
        q = q_ref[:, g * GDH : (g + 1) * GDH].astype(F32)
        out_ref[g, :GDH, :] = q.T.astype(BF16)
        out_ref[g, GDH : GDH + DH, :] = k_ref[g * DH : (g + 1) * DH, :]
        out_ref[g, GDH + DH :, :] = v_ref[g * DH : (g + 1) * DH, :]


def attend_kernel(
    place_ref, q_ref, same_ref, below_ref, above_ref, after_ref, out_ref, kv_buf, k_buf, v_buf, q_buf, sems
):
    z = place_ref[0]
    parity = z % 2
    half = NH // 2
    copies = []
    for c in range(NX):
        copies.append(
            [
                pltpu.make_async_copy(same_ref.at[:, c], kv_buf.at[c, :, parity], sems.at[c, 0]),
                pltpu.make_async_copy(
                    below_ref.at[:, c], kv_buf.at[c, pl.ds(0, half), 1 - parity], sems.at[c, 1]
                ),
                pltpu.make_async_copy(
                    above_ref.at[:, c], kv_buf.at[c, pl.ds(half, half), 1 - parity], sems.at[c, 2]
                ),
            ]
        )
        for copy in copies[c]:
            copy.start()
    scale = math.log2(math.e) / math.sqrt(DH)
    row = lax.broadcasted_iota(jnp.int32, (KEYS, QUERIES), 0)
    col = lax.broadcasted_iota(jnp.int32, (KEYS, QUERIES), 1) % T
    ones = jnp.where(lax.broadcasted_iota(jnp.int32, (16, CHUNK), 0) == 0, 1.0, 0.0).astype(BF16)
    blank = jnp.zeros((128 - DH, T), F32)
    blank_q = jnp.zeros((128 - DH, QUERIES), BF16)
    for c in range(NX):
        q_buf[DH:128, :] = blank_q
        q_buf[128 + DH :, :] = blank_q
        for h in range(GROUP):
            hi, lo = split2(q_ref[c, h * DH : (h + 1) * DH, :].astype(F32) * scale)
            q_buf[:DH, h * T : (h + 1) * T] = hi
            q_buf[128 : 128 + DH, h * T : (h + 1) * T] = lo
        for copy in copies[c]:
            copy.wait()
        v_buf[DH:, c * CHUNK : (c + 1) * CHUNK] = ones
        for b in range(NZ):
            at = slice(c * CHUNK + b * T, c * CHUNK + (b + 1) * T)
            v_buf[:DH, at] = kv_buf[c, b // 2, b % 2, DH:, :]
            k = jnp.concatenate([kv_buf[c, b // 2, b % 2, :DH, :].astype(F32), blank], axis=0).T.astype(BF16)
            k_buf[at, :128] = k
            k_buf[at, 128:] = k
        q = q_buf[...]

        def scores(j, c=c, q=q):
            found = dot(k_buf[j * KEYS : (j + 1) * KEYS, :], q)
            if j * KEYS >= c * CHUNK:
                seen = row + (j * KEYS - c * CHUNK) <= col + z * T
                found = jnp.where(seen, found, masked_score)
            return found

        count = (c + 1) * CHUNK // KEYS
        found = scores(0)
        top = jnp.max(found, axis=0, keepdims=True)
        total = None
        for j in range(count):
            later = scores(j + 1) if j + 1 < count else None
            expos = jnp.exp2(found - top).astype(BF16)
            summed = dot(v_buf[:, j * KEYS : (j + 1) * KEYS], expos)
            total = summed if total is None else total + summed
            if later is not None:
                raised = jnp.maximum(top, jnp.max(later, axis=0, keepdims=True))
                total = total * jnp.exp2(top - raised)
                top = raised
                found = later
        done = (total[:DH, :] / total[DH : DH + 1, :]).astype(BF16)
        for h in range(GROUP):
            out_ref[c, h * DH : (h + 1) * DH, :] = done[:, h * T : (h + 1) * T]


def place_kernel(in_ref, after_ref, out_ref):
    for g in range(KVH):
        out_ref[:, g * GDH : (g + 1) * GDH] = in_ref[g].astype(F32).T.astype(BF16)


VMEM_SPEC = pl.BlockSpec(memory_space=pltpu.VMEM)
SMEM_SPEC = pl.BlockSpec(memory_space=pltpu.SMEM)
ANY_SPEC = pl.BlockSpec(memory_space=pl.ANY)


def call(kernel, shape, specs, scratch=(), limit=48):
    return pl.pallas_call(
        kernel,
        out_shape=jax.ShapeDtypeStruct(shape, BF16),
        in_specs=specs,
        out_specs=VMEM_SPEC,
        scratch_shapes=list(scratch),
        compiler_params=pltpu.CompilerParams(vmem_limit_bytes=limit << 20),
    )


def per_device(mixer_input, input_map, output_map, log_decay, query_rows, key_rows, value_rows):
    place_z = lax.axis_index(("zh", "zl")).astype(jnp.int32).reshape(1)
    place = lax.axis_index(("cx", "zh", "zl")).astype(jnp.int32).reshape(1)
    packed = call(pack_kernel, (KVH, GDH + 2 * DH, T), [VMEM_SPEC] * 3)(
        query_rows, key_rows.T, value_rows.T
    )
    packed = lax.all_to_all(packed, "cx", 0, 0)
    same = lax.all_gather(packed[:, GDH:, :], "zh")
    below = lax.ppermute(same[: NH // 2], ("zh", "zl"), [(k, (k + 1) % NZ) for k in range(NZ)])
    above = lax.ppermute(same[NH // 2 :], ("zh", "zl"), [(k, (k - 1) % NZ) for k in range(NZ)])
    update = call(
        update_kernel, (NCTX, PIECE_ROWS, PIECE_COLS + 128), [VMEM_SPEC] * 3
    )(mixer_input, input_map, log_decay.T)
    update = lax.all_to_all(update, ("cx", "zh", "zl"), 0, 0)
    prefix = call(prefix_kernel, (NCTX, PIECE_ROWS, PIECE_COLS), [SMEM_SPEC, VMEM_SPEC, ANY_SPEC])(
        place, update, same
    )
    entering = lax.all_to_all(prefix, ("cx", "zh", "zl"), 0, 0)
    attended = call(
        attend_kernel,
        (NX, GDH, T),
        [SMEM_SPEC, VMEM_SPEC] + [ANY_SPEC] * 4,
        [
            pltpu.VMEM((NX, NH, 2, 2 * DH, T), BF16),
            pltpu.VMEM((NX * CHUNK, 256), BF16),
            pltpu.VMEM((DH + 16, NX * CHUNK), BF16),
            pltpu.VMEM((256, QUERIES), BF16),
            pltpu.SemaphoreType.DMA((NX, 3)),
        ],
    )(place_z, packed, same, below, above, prefix)
    attended = lax.all_to_all(attended, "cx", 0, 0)
    mixer_output = call(mix_kernel, (T, WIDTH), [VMEM_SPEC] * 5)(
        mixer_input, input_map, output_map, log_decay.T, entering
    )
    attention_output = call(place_kernel, (T, QH * DH), [VMEM_SPEC, VMEM_SPEC])(
        attended, mixer_output[:16, :128]
    )
    return mixer_output, attention_output


def solution(mesh):
    grid = Mesh(mesh.devices.reshape(-1, NX, NH, 2), ("dp", "cx", "zh", "zl"))
    spec = P(("dp", "cx", "zh", "zl"), None)
    return jax.shard_map(
        per_device,
        mesh=grid,
        in_specs=(spec,) * 7,
        out_specs=(spec, spec),
        check_vma=False,
    )
```

```python
import math

import jax
import jax.numpy as jnp
from jax import lax
from jax.experimental import pallas as pl
from jax.experimental.pallas import tpu as pltpu
from jax.sharding import Mesh
from jax.sharding import PartitionSpec as P

MIXER_HEADS = 40
P_SIZE = 64
N = 128
QH = 32
KVH = 4
DH = 80
T = 128
WIDTH = MIXER_HEADS * P_SIZE
GROUP = QH // KVH
GDH = GROUP * DH
NX = 4
NZ = 8
NCTX = NX * NZ
PIECE_ROWS = 16
PIECE_COLS = 640
masked_score = -1e30
F32 = jnp.float32
BF16 = jnp.bfloat16


def split2(a):
    hi = a.astype(BF16)
    return hi, (a - hi.astype(F32)).astype(BF16)


def dot(a, b):
    return jnp.dot(a, b, preferred_element_type=F32)


def dot_nt(a, b):
    return lax.dot_general(a, b, (((1,), (1,)), ((), ())), preferred_element_type=F32)


def head_spread():
    rows = lax.broadcasted_iota(jnp.int32, (MIXER_HEADS, WIDTH), 0)
    cols = lax.broadcasted_iota(jnp.int32, (MIXER_HEADS, WIDTH), 1)
    return jnp.where(cols // P_SIZE == rows, 1.0, 0.0).astype(BF16)


def spread(a, onehot):
    hi, lo = split2(a)
    return dot(hi, onehot) + dot(lo, onehot)


def cumulative_of(decay):
    rows = lax.broadcasted_iota(jnp.int32, (T, T), 0)
    cols = lax.broadcasted_iota(jnp.int32, (T, T), 1)
    lower = jnp.where(cols <= rows, 1.0, 0.0).astype(F32)
    return lax.dot_general(
        lower,
        decay,
        (((1,), (1,)), ((), ())),
        precision=lax.Precision.HIGHEST,
        preferred_element_type=F32,
    )


def update_kernel(x_ref, in_ref, decay_ref, out_ref):
    cumulative = cumulative_of(decay_ref[...])
    last = cumulative[T - 1 : T, :]
    onehot = head_spread()
    tail = spread(jnp.exp(last - cumulative), onehot)
    hi, lo = split2(x_ref[...].astype(F32) * tail)
    in_t = in_ref[...].astype(F32).T.astype(BF16)
    update = (dot(in_t, hi) + dot(in_t, lo)).astype(BF16)
    total = jnp.broadcast_to(jnp.exp(last), (PIECE_ROWS, MIXER_HEADS))
    total_hi, total_lo = split2(total)
    head = lax.broadcasted_iota(jnp.int32, (MIXER_HEADS, 128), 0)
    lane = lax.broadcasted_iota(jnp.int32, (MIXER_HEADS, 128), 1)
    place_hi = jnp.where(lane == head, 1.0, 0.0).astype(BF16)
    place_lo = jnp.where(lane == head + 64, 1.0, 0.0).astype(BF16)
    factor = (dot(total_hi, place_hi) + dot(total_lo, place_lo)).astype(BF16)
    for i in range(N // PIECE_ROWS):
        for j in range(WIDTH // PIECE_COLS):
            d = i * (WIDTH // PIECE_COLS) + j
            out_ref[d, :, :PIECE_COLS] = update[
                i * PIECE_ROWS : (i + 1) * PIECE_ROWS, j * PIECE_COLS : (j + 1) * PIECE_COLS
            ]
            out_ref[d, :, PIECE_COLS:] = factor


def prefix_kernel(place_ref, in_ref, out_ref):
    first_head = (place_ref[0] % (WIDTH // PIECE_COLS)) * (PIECE_COLS // P_SIZE)
    lane = lax.broadcasted_iota(jnp.int32, (128, PIECE_COLS), 0)
    cols = lax.broadcasted_iota(jnp.int32, (128, PIECE_COLS), 1)
    head = first_head + cols // P_SIZE
    onehot = jnp.where((lane == head) | (lane == head + 64), 1.0, 0.0).astype(BF16)
    state = jnp.zeros((PIECE_ROWS, PIECE_COLS), F32)
    for k in range(NCTX):
        out_ref[k] = state.astype(BF16)
        factor = dot(in_ref[k, :, PIECE_COLS:], onehot)
        state = factor * state + in_ref[k, :, :PIECE_COLS].astype(F32)


def mix_kernel(x_ref, in_ref, map_ref, decay_ref, enter_ref, out_ref):
    cumulative = cumulative_of(decay_ref[...])
    middle = 0.5 * cumulative[T - 1 : T, :]
    onehot = head_spread()
    ahead = spread(jnp.exp(cumulative - middle), onehot)
    behind = spread(jnp.exp(middle - cumulative), onehot)
    start = spread(jnp.exp(jnp.broadcast_to(middle, (8, MIXER_HEADS))), onehot)[0:1, :]
    hi, lo = split2(x_ref[...].astype(F32) * behind)
    out_map = map_ref[...]
    match = dot_nt(out_map, in_ref[...])
    rows = lax.broadcasted_iota(jnp.int32, (T, T), 0)
    cols = lax.broadcasted_iota(jnp.int32, (T, T), 1)
    match_hi, match_lo = split2(jnp.where(cols <= rows, match, 0.0))
    inner = dot(match_hi, hi) + dot(match_hi, lo) + dot(match_lo, hi)
    for j in range(WIDTH // PIECE_COLS):
        cut = slice(j * PIECE_COLS, (j + 1) * PIECE_COLS)
        entering = jnp.concatenate(
            [enter_ref[i * (WIDTH // PIECE_COLS) + j] for i in range(N // PIECE_ROWS)], axis=0
        )
        carried = dot(out_map, entering)
        out_ref[:, cut] = (ahead[:, cut] * (inner[:, cut] + start[:, cut] * carried)).astype(BF16)


CHUNK = NZ * T
QUERIES = GROUP * T
KEYS = 512


def pack_kernel(place_ref, q_ref, k_ref, v_ref, *out_refs):
    for step, out_ref in enumerate(out_refs):
        g = (place_ref[0] + step) % NX
        q = q_ref[:, pl.ds(pl.multiple_of(g * GDH, 128), GDH)].astype(F32)
        head = pl.ds(pl.multiple_of(g * DH, 16), DH)
        out_ref[:GDH, :] = q.T.astype(BF16)
        out_ref[GDH : GDH + DH, :] = k_ref[head, :]
        out_ref[GDH + DH :, :] = v_ref[head, :]


def merge_kernel(*refs):
    for s in range(NX):
        refs[NX][s] = refs[s][GDH:, :]


def attend_kernel(place_ref, *refs):
    packs = refs[:NX]
    kv_ref, after_ref, out_ref, q_all, kv_buf, k_buf, v_buf, q_buf, q_sems, kv_sems = refs[NX:]
    x = place_ref[0]
    z = place_ref[1]
    q_copies = [
        pltpu.make_async_copy(
            packs[s].at[pl.ds(0, GDH)], q_all.at[lax.rem(x + (NX - s), NX)], q_sems.at[s]
        )
        for s in range(NX)
    ]
    kv_copies = [
        pltpu.make_async_copy(
            kv_ref.at[:, lax.rem(x + (NX - c), NX)], kv_buf.at[c], kv_sems.at[c]
        )
        for c in range(NX)
    ]
    for copy in q_copies + kv_copies:
        copy.start()
    scale = math.log2(math.e) / math.sqrt(DH)
    row = lax.broadcasted_iota(jnp.int32, (KEYS, QUERIES), 0)
    col = lax.broadcasted_iota(jnp.int32, (KEYS, QUERIES), 1) % T
    ones = jnp.where(lax.broadcasted_iota(jnp.int32, (16, CHUNK), 0) == 0, 1.0, 0.0).astype(BF16)
    blank = jnp.zeros((128 - DH, T), F32)
    blank_q = jnp.zeros((128 - DH, QUERIES), BF16)
    for copy in q_copies:
        copy.wait()
    for c in range(NX):
        q_buf[DH:128, :] = blank_q
        q_buf[128 + DH :, :] = blank_q
        for h in range(GROUP):
            hi, lo = split2(q_all[c, h * DH : (h + 1) * DH, :].astype(F32) * scale)
            q_buf[:DH, h * T : (h + 1) * T] = hi
            q_buf[128 : 128 + DH, h * T : (h + 1) * T] = lo
        kv_copies[c].wait()
        v_buf[DH:, c * CHUNK : (c + 1) * CHUNK] = ones
        for b in range(NZ):
            at = slice(c * CHUNK + b * T, c * CHUNK + (b + 1) * T)
            v_buf[:DH, at] = kv_buf[c, b, DH:, :]
            k = jnp.concatenate([kv_buf[c, b, :DH, :].astype(F32), blank], axis=0).T.astype(BF16)
            k_buf[at, :128] = k
            k_buf[at, 128:] = k
        q = q_buf[...]

        def scores(j, c=c, q=q):
            found = dot(k_buf[j * KEYS : (j + 1) * KEYS, :], q)
            if j * KEYS >= c * CHUNK:
                seen = row + (j * KEYS - c * CHUNK) <= col + z * T
                found = jnp.where(seen, found, masked_score)
            return found

        count = (c + 1) * CHUNK // KEYS
        found = scores(0)
        top = jnp.max(found, axis=0, keepdims=True)
        total = None
        for j in range(count):
            later = scores(j + 1) if j + 1 < count else None
            expos = jnp.exp2(found - top).astype(BF16)
            summed = dot(v_buf[:, j * KEYS : (j + 1) * KEYS], expos)
            total = summed if total is None else total + summed
            if later is not None:
                raised = jnp.maximum(top, jnp.max(later, axis=0, keepdims=True))
                total = total * jnp.exp2(top - raised)
                top = raised
                found = later
        done = (total[:DH, :] / total[DH : DH + 1, :]).astype(BF16)
        for h in range(GROUP):
            out_ref[c, h * DH : (h + 1) * DH, :] = done[:, h * T : (h + 1) * T]


def place_kernel(in_ref, after_ref, out_ref):
    for g in range(KVH):
        out_ref[:, g * GDH : (g + 1) * GDH] = in_ref[g].astype(F32).T.astype(BF16)


VMEM_SPEC = pl.BlockSpec(memory_space=pltpu.VMEM)
SMEM_SPEC = pl.BlockSpec(memory_space=pltpu.SMEM)
ANY_SPEC = pl.BlockSpec(memory_space=pl.ANY)


def call(kernel, shape, specs, scratch=(), limit=48):
    return pl.pallas_call(
        kernel,
        out_shape=jax.ShapeDtypeStruct(shape, BF16),
        in_specs=specs,
        out_specs=VMEM_SPEC,
        scratch_shapes=list(scratch),
        compiler_params=pltpu.CompilerParams(vmem_limit_bytes=limit << 20),
    )


def per_device(mixer_input, input_map, output_map, log_decay, query_rows, key_rows, value_rows):
    x = lax.axis_index("cx").astype(jnp.int32)
    z = lax.axis_index("cz").astype(jnp.int32)
    place_xz = jnp.stack([x, z])
    place = (x * NZ + z).reshape(1)
    packs = pl.pallas_call(
        pack_kernel,
        out_shape=[jax.ShapeDtypeStruct((GDH + 2 * DH, T), BF16)] * NX,
        in_specs=[SMEM_SPEC] + [VMEM_SPEC] * 3,
        out_specs=[VMEM_SPEC] * NX,
    )(place_xz, query_rows, key_rows.T, value_rows.T)
    packs = [packs[0]] + [
        lax.ppermute(packs[s], "cx", [(k, (k + s) % NX) for k in range(NX)])
        for s in range(1, NX)
    ]
    kv = lax.all_gather(call(merge_kernel, (NX, 2 * DH, T), [VMEM_SPEC] * NX)(*packs), "cz")
    update = call(
        update_kernel, (NCTX, PIECE_ROWS, PIECE_COLS + 128), [VMEM_SPEC] * 3
    )(mixer_input, input_map, log_decay.T)
    update = lax.all_to_all(update, ("cx", "cz"), 0, 0)
    prefix = call(prefix_kernel, (NCTX, PIECE_ROWS, PIECE_COLS), [SMEM_SPEC, VMEM_SPEC])(
        place, update
    )
    entering = lax.all_to_all(prefix, ("cx", "cz"), 0, 0)
    attended = call(
        attend_kernel,
        (NX, GDH, T),
        [SMEM_SPEC] + [ANY_SPEC] * (NX + 2),
        [
            pltpu.VMEM((NX, GDH, T), BF16),
            pltpu.VMEM((NX, NZ, 2 * DH, T), BF16),
            pltpu.VMEM((NX * CHUNK, 256), BF16),
            pltpu.VMEM((DH + 16, NX * CHUNK), BF16),
            pltpu.VMEM((256, QUERIES), BF16),
            pltpu.SemaphoreType.DMA((NX,)),
            pltpu.SemaphoreType.DMA((NX,)),
        ],
    )(place_xz, *packs, kv, prefix)
    attended = lax.all_to_all(attended, "cx", 0, 0)
    mixer_output = call(mix_kernel, (T, WIDTH), [VMEM_SPEC] * 5)(
        mixer_input, input_map, output_map, log_decay.T, entering
    )
    attention_output = call(place_kernel, (T, QH * DH), [VMEM_SPEC, VMEM_SPEC])(
        attended, mixer_output[:16, :128]
    )
    return mixer_output, attention_output


def solution(mesh):
    grid = Mesh(mesh.devices.reshape(-1, NX, NZ), ("dp", "cx", "cz"))
    spec = P(("dp", "cx", "cz"), None)
    return jax.shard_map(
        per_device,
        mesh=grid,
        in_specs=(spec,) * 7,
        out_specs=(spec, spec),
        check_vma=False,
    )
```

```python
import math

import jax
import jax.numpy as jnp
from jax import lax
from jax.experimental import pallas as pl
from jax.experimental.pallas import tpu as pltpu
from jax.sharding import Mesh
from jax.sharding import PartitionSpec as P

MIXER_HEADS = 40
P_SIZE = 64
N = 128
QH = 32
KVH = 4
DH = 80
T = 128
WIDTH = MIXER_HEADS * P_SIZE
GROUP = QH // KVH
GDH = GROUP * DH
NX = 4
NH = 4
NZ = 2 * NH
NCTX = NX * NZ
PIECE_ROWS = 16
PIECE_COLS = 640
masked_score = -1e30
F32 = jnp.float32
BF16 = jnp.bfloat16


def split2(a):
    hi = a.astype(BF16)
    return hi, (a - hi.astype(F32)).astype(BF16)


def dot(a, b):
    return jnp.dot(a, b, preferred_element_type=F32)


def dot_nt(a, b):
    return lax.dot_general(a, b, (((1,), (1,)), ((), ())), preferred_element_type=F32)


def head_spread():
    rows = lax.broadcasted_iota(jnp.int32, (MIXER_HEADS, WIDTH), 0)
    cols = lax.broadcasted_iota(jnp.int32, (MIXER_HEADS, WIDTH), 1)
    return jnp.where(cols // P_SIZE == rows, 1.0, 0.0).astype(BF16)


def spread(a, onehot):
    hi, lo = split2(a)
    return dot(hi, onehot) + dot(lo, onehot)


def cumulative_of(decay):
    rows = lax.broadcasted_iota(jnp.int32, (T, T), 0)
    cols = lax.broadcasted_iota(jnp.int32, (T, T), 1)
    lower = jnp.where(cols <= rows, 1.0, 0.0).astype(F32)
    return lax.dot_general(
        lower,
        decay,
        (((1,), (1,)), ((), ())),
        precision=lax.Precision.HIGHEST,
        preferred_element_type=F32,
    )


def update_kernel(x_ref, in_ref, decay_ref, after_ref, out_ref):
    cumulative = cumulative_of(decay_ref[...])
    last = cumulative[T - 1 : T, :]
    onehot = head_spread()
    tail = spread(jnp.exp(last - cumulative), onehot)
    hi, lo = split2(x_ref[...].astype(F32) * tail)
    in_t = in_ref[...].astype(F32).T.astype(BF16)
    update = (dot(in_t, hi) + dot(in_t, lo)).astype(BF16)
    total = jnp.broadcast_to(jnp.exp(last), (PIECE_ROWS, MIXER_HEADS))
    total_hi, total_lo = split2(total)
    head = lax.broadcasted_iota(jnp.int32, (MIXER_HEADS, 128), 0)
    lane = lax.broadcasted_iota(jnp.int32, (MIXER_HEADS, 128), 1)
    place_hi = jnp.where(lane == head, 1.0, 0.0).astype(BF16)
    place_lo = jnp.where(lane == head + 64, 1.0, 0.0).astype(BF16)
    factor = (dot(total_hi, place_hi) + dot(total_lo, place_lo)).astype(BF16)
    for i in range(N // PIECE_ROWS):
        for j in range(WIDTH // PIECE_COLS):
            d = i * (WIDTH // PIECE_COLS) + j
            out_ref[d, :, :PIECE_COLS] = update[
                i * PIECE_ROWS : (i + 1) * PIECE_ROWS, j * PIECE_COLS : (j + 1) * PIECE_COLS
            ]
            out_ref[d, :, PIECE_COLS:] = factor


def prefix_kernel(place_ref, in_ref, after_ref, below_ref, above_ref, out_ref):
    first_head = (place_ref[0] % (WIDTH // PIECE_COLS)) * (PIECE_COLS // P_SIZE)
    lane = lax.broadcasted_iota(jnp.int32, (128, PIECE_COLS), 0)
    cols = lax.broadcasted_iota(jnp.int32, (128, PIECE_COLS), 1)
    head = first_head + cols // P_SIZE
    onehot = jnp.where((lane == head) | (lane == head + 64), 1.0, 0.0).astype(BF16)
    state = jnp.zeros((PIECE_ROWS, PIECE_COLS), F32)
    for k in range(NCTX):
        out_ref[k] = state.astype(BF16)
        factor = dot(in_ref[k, :, PIECE_COLS:], onehot)
        state = factor * state + in_ref[k, :, :PIECE_COLS].astype(F32)


def mix_kernel(x_ref, in_ref, map_ref, decay_ref, enter_ref, out_ref):
    cumulative = cumulative_of(decay_ref[...])
    middle = 0.5 * cumulative[T - 1 : T, :]
    onehot = head_spread()
    ahead = spread(jnp.exp(cumulative - middle), onehot)
    behind = spread(jnp.exp(middle - cumulative), onehot)
    start = spread(jnp.exp(jnp.broadcast_to(middle, (8, MIXER_HEADS))), onehot)[0:1, :]
    hi, lo = split2(x_ref[...].astype(F32) * behind)
    out_map = map_ref[...]
    match = dot_nt(out_map, in_ref[...])
    rows = lax.broadcasted_iota(jnp.int32, (T, T), 0)
    cols = lax.broadcasted_iota(jnp.int32, (T, T), 1)
    match_hi, match_lo = split2(jnp.where(cols <= rows, match, 0.0))
    inner = dot(match_hi, hi) + dot(match_hi, lo) + dot(match_lo, hi)
    for j in range(WIDTH // PIECE_COLS):
        cut = slice(j * PIECE_COLS, (j + 1) * PIECE_COLS)
        entering = jnp.concatenate(
            [enter_ref[i * (WIDTH // PIECE_COLS) + j] for i in range(N // PIECE_ROWS)], axis=0
        )
        carried = dot(out_map, entering)
        out_ref[:, cut] = (ahead[:, cut] * (inner[:, cut] + start[:, cut] * carried)).astype(BF16)


QUERIES = GROUP * T
KEYS = NH * T


def pack_kernel(q_ref, k_ref, v_ref, out_ref):
    for g in range(KVH):
        q = q_ref[:, g * GDH : (g + 1) * GDH].astype(F32)
        out_ref[g, :GDH, :] = q.T.astype(BF16)
        out_ref[g, GDH : GDH + DH, :] = k_ref[g * DH : (g + 1) * DH, :]
        out_ref[g, GDH + DH :, :] = v_ref[g * DH : (g + 1) * DH, :]


def attend(place_ref, q_ref, block, parity, k_buf, v_buf, q_buf, begin, end):
    z = place_ref[0]
    scale = math.log2(math.e) / math.sqrt(DH)
    row = lax.broadcasted_iota(jnp.int32, (KEYS, QUERIES), 0)
    row = row + row // T * T + parity * T
    col = lax.broadcasted_iota(jnp.int32, (KEYS, QUERIES), 1) % T
    ones = jnp.where(lax.broadcasted_iota(jnp.int32, (16, KEYS), 0) == 0, 1.0, 0.0).astype(BF16)
    blank = jnp.zeros((128 - DH, T), F32)
    blank_q = jnp.zeros((128 - DH, QUERIES), BF16)
    for c in range(NX):
        q_buf[DH:128, :] = blank_q
        q_buf[128 + DH :, :] = blank_q
        for h in range(GROUP):
            hi, lo = split2(q_ref[c, h * DH : (h + 1) * DH, :].astype(F32) * scale)
            q_buf[:DH, h * T : (h + 1) * T] = hi
            q_buf[128 : 128 + DH, h * T : (h + 1) * T] = lo
        v_buf[DH:, c * KEYS : (c + 1) * KEYS] = ones
        for i in range(NH):
            at = slice(c * KEYS + i * T, c * KEYS + (i + 1) * T)
            kv = block(c, i)
            v_buf[:DH, at] = kv[DH:, :]
            k = jnp.concatenate([kv[:DH, :].astype(F32), blank], axis=0).T.astype(BF16)
            k_buf[at, :128] = k
            k_buf[at, 128:] = k
        q = q_buf[...]

        def scores(j, c=c, q=q):
            found = dot(k_buf[j * KEYS : (j + 1) * KEYS, :], q)
            if j == c:
                found = jnp.where(row <= col + z * T, found, masked_score)
            return found

        total, top = begin(c)
        found = scores(0)
        for j in range(c + 1):
            later = scores(j + 1) if j < c else None
            highest = jnp.max(found, axis=0, keepdims=True)
            if top is None:
                top = highest
            else:
                raised = jnp.maximum(top, highest)
                total = total * jnp.exp2(top - raised)
                top = raised
            expos = jnp.exp2(found - top).astype(BF16)
            summed = dot(v_buf[:, j * KEYS : (j + 1) * KEYS], expos)
            total = summed if total is None else total + summed
            found = later
        end(c, total, top)


def attend_same_kernel(place_ref, q_ref, same_ref, total_ref, top_ref, *bufs):
    def end(c, total, top):
        total_ref[c] = total
        top_ref[c] = top

    attend(
        place_ref,
        q_ref,
        lambda c, i: same_ref[i, c],
        place_ref[0] % 2,
        *bufs,
        lambda c: (None, None),
        end,
    )


def attend_other_kernel(
    place_ref, q_ref, below_ref, above_ref, total_ref, top_ref, after_ref, out_ref, *bufs
):
    def end(c, total, top):
        done = (total[:DH, :] / total[DH : DH + 1, :]).astype(BF16)
        for h in range(GROUP):
            out_ref[c, h * DH : (h + 1) * DH, :] = done[:, h * T : (h + 1) * T]

    half = NH // 2
    attend(
        place_ref,
        q_ref,
        lambda c, i: below_ref[i, c] if i < half else above_ref[i - half, c],
        1 - place_ref[0] % 2,
        *bufs,
        lambda c: (total_ref[c], top_ref[c]),
        end,
    )


def place_kernel(in_ref, after_ref, out_ref):
    for g in range(KVH):
        out_ref[:, g * GDH : (g + 1) * GDH] = in_ref[g].astype(F32).T.astype(BF16)


VMEM_SPEC = pl.BlockSpec(memory_space=pltpu.VMEM)
SMEM_SPEC = pl.BlockSpec(memory_space=pltpu.SMEM)
ANY_SPEC = pl.BlockSpec(memory_space=pl.ANY)


def call(kernel, shape, specs, scratch=(), limit=24):
    return pl.pallas_call(
        kernel,
        out_shape=jax.ShapeDtypeStruct(shape, BF16),
        in_specs=specs,
        out_specs=VMEM_SPEC,
        scratch_shapes=list(scratch),
        compiler_params=pltpu.CompilerParams(vmem_limit_bytes=limit << 20),
    )


def per_device(mixer_input, input_map, output_map, log_decay, query_rows, key_rows, value_rows):
    place_z = lax.axis_index(("zh", "zl")).astype(jnp.int32).reshape(1)
    place = lax.axis_index(("cx", "zh", "zl")).astype(jnp.int32).reshape(1)
    packed = call(pack_kernel, (KVH, GDH + 2 * DH, T), [VMEM_SPEC] * 3)(
        query_rows, key_rows.T, value_rows.T
    )
    packed = lax.all_to_all(packed, "cx", 0, 0)
    same = lax.all_gather(packed[:, GDH:, :], "zh")
    below = lax.ppermute(same[: NH // 2], ("zh", "zl"), [(k, (k + 1) % NZ) for k in range(NZ)])
    above = lax.ppermute(same[NH // 2 :], ("zh", "zl"), [(k, (k - 1) % NZ) for k in range(NZ)])
    update = call(
        update_kernel, (NCTX, PIECE_ROWS, PIECE_COLS + 128), [VMEM_SPEC] * 3 + [ANY_SPEC]
    )(mixer_input, input_map, log_decay.T, same)
    update = lax.all_to_all(update, ("cx", "zh", "zl"), 0, 0)
    bufs = [
        pltpu.VMEM((NX * KEYS, 256), BF16),
        pltpu.VMEM((DH + 16, NX * KEYS), BF16),
        pltpu.VMEM((256, QUERIES), BF16),
    ]
    total, top = pl.pallas_call(
        attend_same_kernel,
        out_shape=[
            jax.ShapeDtypeStruct((NX, DH + 16, QUERIES), F32),
            jax.ShapeDtypeStruct((NX, 1, QUERIES), F32),
        ],
        in_specs=[SMEM_SPEC, VMEM_SPEC, VMEM_SPEC],
        out_specs=[VMEM_SPEC, VMEM_SPEC],
        scratch_shapes=bufs,
        compiler_params=pltpu.CompilerParams(vmem_limit_bytes=24 << 20),
    )(place_z, packed, same)
    prefix = call(
        prefix_kernel,
        (NCTX, PIECE_ROWS, PIECE_COLS),
        [SMEM_SPEC, VMEM_SPEC, VMEM_SPEC, ANY_SPEC, ANY_SPEC],
    )(place, update, top, below, above)
    entering = lax.all_to_all(prefix, ("cx", "zh", "zl"), 0, 0)
    attended = call(
        attend_other_kernel, (NX, GDH, T), [SMEM_SPEC] + [VMEM_SPEC] * 5 + [ANY_SPEC], bufs
    )(place_z, packed, below, above, total, top, prefix)
    attended = lax.all_to_all(attended, "cx", 0, 0)
    mixer_output = call(mix_kernel, (T, WIDTH), [VMEM_SPEC] * 5)(
        mixer_input, input_map, output_map, log_decay.T, entering
    )
    attention_output = call(place_kernel, (T, QH * DH), [VMEM_SPEC, VMEM_SPEC])(
        attended, mixer_output[:16, :128]
    )
    return mixer_output, attention_output


def solution(mesh):
    grid = Mesh(mesh.devices.reshape(-1, NX, NH, 2), ("dp", "cx", "zh", "zl"))
    spec = P(("dp", "cx", "zh", "zl"), None)
    return jax.shard_map(
        per_device,
        mesh=grid,
        in_specs=(spec,) * 7,
        out_specs=(spec, spec),
        check_vma=False,
    )
```

```python
import math

import jax
import jax.numpy as jnp
from jax import lax
from jax.experimental import pallas as pl
from jax.experimental.pallas import tpu as pltpu
from jax.sharding import Mesh
from jax.sharding import PartitionSpec as P

MIXER_HEADS = 40
P_SIZE = 64
N = 128
QH = 32
KVH = 4
DH = 80
T = 128
WIDTH = MIXER_HEADS * P_SIZE
GROUP = QH // KVH
GDH = GROUP * DH
NX = 4
NH = 4
NZ = 2 * NH
NCTX = NX * NZ
PIECE_ROWS = 16
PIECE_COLS = 640
masked_score = -1e30
F32 = jnp.float32
BF16 = jnp.bfloat16


def split2(a):
    hi = a.astype(BF16)
    return hi, (a - hi.astype(F32)).astype(BF16)


def dot(a, b):
    return jnp.dot(a, b, preferred_element_type=F32)


def dot_nt(a, b):
    return lax.dot_general(a, b, (((1,), (1,)), ((), ())), preferred_element_type=F32)


def head_spread():
    rows = lax.broadcasted_iota(jnp.int32, (MIXER_HEADS, WIDTH), 0)
    cols = lax.broadcasted_iota(jnp.int32, (MIXER_HEADS, WIDTH), 1)
    return jnp.where(cols // P_SIZE == rows, 1.0, 0.0).astype(BF16)


def spread(a, onehot):
    hi, lo = split2(a)
    return dot(hi, onehot) + dot(lo, onehot)


def cumulative_of(decay):
    rows = lax.broadcasted_iota(jnp.int32, (T, T), 0)
    cols = lax.broadcasted_iota(jnp.int32, (T, T), 1)
    lower = jnp.where(cols <= rows, 1.0, 0.0).astype(F32)
    return lax.dot_general(
        lower,
        decay,
        (((1,), (1,)), ((), ())),
        precision=lax.Precision.HIGHEST,
        preferred_element_type=F32,
    )


def update_kernel(x_ref, in_ref, decay_ref, after_ref, out_ref):
    cumulative = cumulative_of(decay_ref[...])
    last = cumulative[T - 1 : T, :]
    onehot = head_spread()
    tail = spread(jnp.exp(last - cumulative), onehot)
    hi, lo = split2(x_ref[...].astype(F32) * tail)
    in_t = in_ref[...].astype(F32).T.astype(BF16)
    update = (dot(in_t, hi) + dot(in_t, lo)).astype(BF16)
    total = jnp.broadcast_to(jnp.exp(last), (PIECE_ROWS, MIXER_HEADS))
    total_hi, total_lo = split2(total)
    head = lax.broadcasted_iota(jnp.int32, (MIXER_HEADS, 128), 0)
    lane = lax.broadcasted_iota(jnp.int32, (MIXER_HEADS, 128), 1)
    place_hi = jnp.where(lane == head, 1.0, 0.0).astype(BF16)
    place_lo = jnp.where(lane == head + 64, 1.0, 0.0).astype(BF16)
    factor = (dot(total_hi, place_hi) + dot(total_lo, place_lo)).astype(BF16)
    for i in range(N // PIECE_ROWS):
        for j in range(WIDTH // PIECE_COLS):
            d = i * (WIDTH // PIECE_COLS) + j
            out_ref[d, :, :PIECE_COLS] = update[
                i * PIECE_ROWS : (i + 1) * PIECE_ROWS, j * PIECE_COLS : (j + 1) * PIECE_COLS
            ]
            out_ref[d, :, PIECE_COLS:] = factor


def prefix_kernel(place_ref, in_ref, after_ref, below_ref, above_ref, out_ref):
    first_head = (place_ref[0] % (WIDTH // PIECE_COLS)) * (PIECE_COLS // P_SIZE)
    lane = lax.broadcasted_iota(jnp.int32, (128, PIECE_COLS), 0)
    cols = lax.broadcasted_iota(jnp.int32, (128, PIECE_COLS), 1)
    head = first_head + cols // P_SIZE
    onehot = jnp.where((lane == head) | (lane == head + 64), 1.0, 0.0).astype(BF16)
    state = jnp.zeros((PIECE_ROWS, PIECE_COLS), F32)
    for k in range(NCTX):
        out_ref[k] = state.astype(BF16)
        factor = dot(in_ref[k, :, PIECE_COLS:], onehot)
        state = factor * state + in_ref[k, :, :PIECE_COLS].astype(F32)


def mix_kernel(x_ref, in_ref, map_ref, decay_ref, enter_ref, out_ref):
    cumulative = cumulative_of(decay_ref[...])
    middle = 0.5 * cumulative[T - 1 : T, :]
    onehot = head_spread()
    ahead = spread(jnp.exp(cumulative - middle), onehot)
    behind = spread(jnp.exp(middle - cumulative), onehot)
    start = spread(jnp.exp(jnp.broadcast_to(middle, (8, MIXER_HEADS))), onehot)[0:1, :]
    hi, lo = split2(x_ref[...].astype(F32) * behind)
    out_map = map_ref[...]
    match = dot_nt(out_map, in_ref[...])
    rows = lax.broadcasted_iota(jnp.int32, (T, T), 0)
    cols = lax.broadcasted_iota(jnp.int32, (T, T), 1)
    match_hi, match_lo = split2(jnp.where(cols <= rows, match, 0.0))
    inner = dot(match_hi, hi) + dot(match_hi, lo) + dot(match_lo, hi)
    for j in range(WIDTH // PIECE_COLS):
        cut = slice(j * PIECE_COLS, (j + 1) * PIECE_COLS)
        entering = jnp.concatenate(
            [enter_ref[i * (WIDTH // PIECE_COLS) + j] for i in range(N // PIECE_ROWS)], axis=0
        )
        carried = dot(out_map, entering)
        out_ref[:, cut] = (ahead[:, cut] * (inner[:, cut] + start[:, cut] * carried)).astype(BF16)


QUERIES = GROUP * T
KEYS = NH * T


def pack_kernel(k_ref, v_ref, out_ref):
    for g in range(KVH):
        for i in range(NH):
            out_ref[i * NX + g, :DH, :] = k_ref[g * DH : (g + 1) * DH, :]
            out_ref[i * NX + g, DH:, :] = v_ref[g * DH : (g + 1) * DH, :]


def turn_kernel(place_ref, q_ref, *out_refs):
    for step, out_ref in enumerate(out_refs):
        g = lax.rem(place_ref[0] + step, NX)
        q = q_ref[:, pl.ds(pl.multiple_of(g * GDH, 128), GDH)].astype(F32)
        out_ref[...] = q.T.astype(BF16)


def scale_kernel(place_ref, *refs):
    scale = math.log2(math.e) / math.sqrt(DH)
    out_ref = refs[NX]
    blank = jnp.zeros((128 - DH, QUERIES), BF16)
    for s in range(NX):
        c = lax.rem(place_ref[0] + (NX - s), NX)
        out_ref[c, DH:128, :] = blank
        out_ref[c, 128 + DH :, :] = blank
        for h in range(GROUP):
            hi, lo = split2(refs[s][h * DH : (h + 1) * DH, :].astype(F32) * scale)
            out_ref[c, :DH, h * T : (h + 1) * T] = hi
            out_ref[c, 128 : 128 + DH, h * T : (h + 1) * T] = lo


def attend(place_ref, q_ref, block, parity, k_buf, v_buf, begin, end):
    z = place_ref[0]
    row = lax.broadcasted_iota(jnp.int32, (KEYS, QUERIES), 0)
    row = row + row // T * T + parity * T
    col = lax.broadcasted_iota(jnp.int32, (KEYS, QUERIES), 1) % T
    ones = jnp.where(lax.broadcasted_iota(jnp.int32, (16, KEYS), 0) == 0, 1.0, 0.0).astype(BF16)
    blank = jnp.zeros((128 - DH, T), F32)
    for c in range(NX):
        v_buf[DH:, c * KEYS : (c + 1) * KEYS] = ones
        for i in range(NH):
            at = slice(c * KEYS + i * T, c * KEYS + (i + 1) * T)
            kv = block(c, i)
            v_buf[:DH, at] = kv[DH:, :]
            k = jnp.concatenate([kv[:DH, :].astype(F32), blank], axis=0).T.astype(BF16)
            k_buf[at, :128] = k
            k_buf[at, 128:] = k
        q = q_ref[c]

        def scores(j, c=c, q=q):
            found = dot(k_buf[j * KEYS : (j + 1) * KEYS, :], q)
            if j == c:
                found = jnp.where(row <= col + z * T, found, masked_score)
            return found

        total, top = begin(c)
        found = scores(0)
        for j in range(c + 1):
            later = scores(j + 1) if j < c else None
            highest = jnp.max(found, axis=0, keepdims=True)
            if top is None:
                top = highest
            else:
                raised = jnp.maximum(top, highest)
                total = total * jnp.exp2(top - raised)
                top = raised
            expos = jnp.exp2(found - top).astype(BF16)
            summed = dot(v_buf[:, j * KEYS : (j + 1) * KEYS], expos)
            total = summed if total is None else total + summed
            found = later
        end(c, total, top)


def attend_same_kernel(place_ref, q_ref, same_ref, total_ref, top_ref, *bufs):
    def end(c, total, top):
        total_ref[c] = total
        top_ref[c] = top

    attend(
        place_ref,
        q_ref,
        lambda c, i: same_ref[i * NX + c],
        place_ref[0] % 2,
        *bufs,
        lambda c: (None, None),
        end,
    )


def attend_other_kernel(
    place_ref, q_ref, below_ref, above_ref, total_ref, top_ref, after_ref, out_ref, *bufs
):
    def end(c, total, top):
        done = (total[:DH, :] / total[DH : DH + 1, :]).astype(BF16)
        for h in range(GROUP):
            out_ref[c, h * DH : (h + 1) * DH, :] = done[:, h * T : (h + 1) * T]

    half = NH // 2
    attend(
        place_ref,
        q_ref,
        lambda c, i: (
            below_ref[i * NX + c] if i < half else above_ref[(i - half) * NX + c]
        ),
        1 - place_ref[0] % 2,
        *bufs,
        lambda c: (total_ref[c], top_ref[c]),
        end,
    )


def place_kernel(in_ref, after_ref, out_ref):
    for g in range(KVH):
        out_ref[:, g * GDH : (g + 1) * GDH] = in_ref[g].astype(F32).T.astype(BF16)


VMEM_SPEC = pl.BlockSpec(memory_space=pltpu.VMEM)
SMEM_SPEC = pl.BlockSpec(memory_space=pltpu.SMEM)
ANY_SPEC = pl.BlockSpec(memory_space=pl.ANY)


def call(kernel, shape, specs, scratch=(), limit=24):
    return pl.pallas_call(
        kernel,
        out_shape=jax.ShapeDtypeStruct(shape, BF16),
        in_specs=specs,
        out_specs=VMEM_SPEC,
        scratch_shapes=list(scratch),
        compiler_params=pltpu.CompilerParams(vmem_limit_bytes=limit << 20),
    )


def per_device(mixer_input, input_map, output_map, log_decay, query_rows, key_rows, value_rows):
    x = lax.axis_index("cx").astype(jnp.int32).reshape(1)
    z = lax.axis_index(("zh", "zl")).astype(jnp.int32).reshape(1)
    place = x * NZ + z
    pack = call(pack_kernel, (NH * NX, 2 * DH, T), [VMEM_SPEC] * 2)(key_rows.T, value_rows.T)
    same = lax.all_to_all(pack, ("zh", "cx"), 0, 0)
    half = NH * NX // 2
    below = lax.ppermute(same[:half], ("zh", "zl"), [(k, (k + 1) % NZ) for k in range(NZ)])
    above = lax.ppermute(same[half:], ("zh", "zl"), [(k, (k - 1) % NZ) for k in range(NZ)])
    turned = pl.pallas_call(
        turn_kernel,
        out_shape=[jax.ShapeDtypeStruct((GDH, T), BF16)] * NX,
        in_specs=[SMEM_SPEC, VMEM_SPEC],
        out_specs=[VMEM_SPEC] * NX,
    )(x, query_rows)
    turned = [turned[0]] + [
        lax.ppermute(turned[s], "cx", [(k, (k + s) % NX) for k in range(NX)])
        for s in range(1, NX)
    ]
    queries = call(scale_kernel, (NX, 256, QUERIES), [SMEM_SPEC] + [VMEM_SPEC] * NX)(x, *turned)
    update = call(
        update_kernel, (NCTX, PIECE_ROWS, PIECE_COLS + 128), [VMEM_SPEC] * 3 + [ANY_SPEC]
    )(mixer_input, input_map, log_decay.T, queries)
    update = lax.all_to_all(update, ("cx", "zh", "zl"), 0, 0)
    bufs = [
        pltpu.VMEM((NX * KEYS, 256), BF16),
        pltpu.VMEM((DH + 16, NX * KEYS), BF16),
    ]
    total, top = pl.pallas_call(
        attend_same_kernel,
        out_shape=[
            jax.ShapeDtypeStruct((NX, DH + 16, QUERIES), F32),
            jax.ShapeDtypeStruct((NX, 1, QUERIES), F32),
        ],
        in_specs=[SMEM_SPEC, VMEM_SPEC, VMEM_SPEC],
        out_specs=[VMEM_SPEC, VMEM_SPEC],
        scratch_shapes=bufs,
        compiler_params=pltpu.CompilerParams(vmem_limit_bytes=24 << 20),
    )(z, queries, same)
    prefix = call(
        prefix_kernel,
        (NCTX, PIECE_ROWS, PIECE_COLS),
        [SMEM_SPEC, VMEM_SPEC, VMEM_SPEC, ANY_SPEC, ANY_SPEC],
    )(place, update, top, below, above)
    entering = lax.all_to_all(prefix, ("cx", "zh", "zl"), 0, 0)
    attended = call(
        attend_other_kernel, (NX, GDH, T), [SMEM_SPEC] + [VMEM_SPEC] * 5 + [ANY_SPEC], bufs
    )(z, queries, below, above, total, top, prefix)
    attended = lax.all_to_all(attended, "cx", 0, 0)
    mixer_output = call(mix_kernel, (T, WIDTH), [VMEM_SPEC] * 5)(
        mixer_input, input_map, output_map, log_decay.T, entering
    )
    attention_output = call(place_kernel, (T, QH * DH), [VMEM_SPEC, VMEM_SPEC])(
        attended, mixer_output[:16, :128]
    )
    return mixer_output, attention_output


def solution(mesh):
    grid = Mesh(mesh.devices.reshape(-1, NX, NH, 2), ("dp", "cx", "zh", "zl"))
    spec = P(("dp", "cx", "zh", "zl"), None)
    return jax.shard_map(
        per_device,
        mesh=grid,
        in_specs=(spec,) * 7,
        out_specs=(spec, spec),
        check_vma=False,
    )
```

```python
import math

import jax
import jax.numpy as jnp
from jax import lax
from jax.experimental import pallas as pl
from jax.experimental.pallas import tpu as pltpu
from jax.sharding import Mesh
from jax.sharding import PartitionSpec as P

MIXER_HEADS = 40
P_SIZE = 64
N = 128
QH = 32
KVH = 4
DH = 80
T = 128
WIDTH = MIXER_HEADS * P_SIZE
GROUP = QH // KVH
GDH = GROUP * DH
NX = 4
NH = 4
NZ = 2 * NH
NCTX = NX * NZ
PIECE_ROWS = 16
PIECE_COLS = 640
masked_score = -1e30
F32 = jnp.float32
BF16 = jnp.bfloat16


def split2(a):
    hi = a.astype(BF16)
    return hi, (a - hi.astype(F32)).astype(BF16)


def dot(a, b):
    return jnp.dot(a, b, preferred_element_type=F32)


def dot_nt(a, b):
    return lax.dot_general(a, b, (((1,), (1,)), ((), ())), preferred_element_type=F32)


def head_spread():
    rows = lax.broadcasted_iota(jnp.int32, (MIXER_HEADS, WIDTH), 0)
    cols = lax.broadcasted_iota(jnp.int32, (MIXER_HEADS, WIDTH), 1)
    return jnp.where(cols // P_SIZE == rows, 1.0, 0.0).astype(BF16)


def spread(a, onehot):
    hi, lo = split2(a)
    return dot(hi, onehot) + dot(lo, onehot)


def cumulative_of(decay):
    rows = lax.broadcasted_iota(jnp.int32, (T, T), 0)
    cols = lax.broadcasted_iota(jnp.int32, (T, T), 1)
    lower = jnp.where(cols <= rows, 1.0, 0.0).astype(F32)
    return lax.dot_general(
        lower,
        decay,
        (((1,), (1,)), ((), ())),
        precision=lax.Precision.HIGHEST,
        preferred_element_type=F32,
    )


def update_kernel(x_ref, in_ref, decay_ref, out_ref):
    cumulative = cumulative_of(decay_ref[...])
    last = cumulative[T - 1 : T, :]
    onehot = head_spread()
    tail = spread(jnp.exp(last - cumulative), onehot)
    hi, lo = split2(x_ref[...].astype(F32) * tail)
    in_t = in_ref[...].astype(F32).T.astype(BF16)
    update = (dot(in_t, hi) + dot(in_t, lo)).astype(BF16)
    total = jnp.broadcast_to(jnp.exp(last), (PIECE_ROWS, MIXER_HEADS))
    total_hi, total_lo = split2(total)
    head = lax.broadcasted_iota(jnp.int32, (MIXER_HEADS, 128), 0)
    lane = lax.broadcasted_iota(jnp.int32, (MIXER_HEADS, 128), 1)
    place_hi = jnp.where(lane == head, 1.0, 0.0).astype(BF16)
    place_lo = jnp.where(lane == head + 64, 1.0, 0.0).astype(BF16)
    factor = (dot(total_hi, place_hi) + dot(total_lo, place_lo)).astype(BF16)
    for i in range(N // PIECE_ROWS):
        for j in range(WIDTH // PIECE_COLS):
            d = i * (WIDTH // PIECE_COLS) + j
            out_ref[d, :, :PIECE_COLS] = update[
                i * PIECE_ROWS : (i + 1) * PIECE_ROWS, j * PIECE_COLS : (j + 1) * PIECE_COLS
            ]
            out_ref[d, :, PIECE_COLS:] = factor


def prefix_kernel(place_ref, in_ref, after_ref, out_ref):
    first_head = (place_ref[0] % (WIDTH // PIECE_COLS)) * (PIECE_COLS // P_SIZE)
    lane = lax.broadcasted_iota(jnp.int32, (128, PIECE_COLS), 0)
    cols = lax.broadcasted_iota(jnp.int32, (128, PIECE_COLS), 1)
    head = first_head + cols // P_SIZE
    onehot = jnp.where((lane == head) | (lane == head + 64), 1.0, 0.0).astype(BF16)
    state = jnp.zeros((PIECE_ROWS, PIECE_COLS), F32)
    for k in range(NCTX):
        out_ref[k] = state.astype(BF16)
        factor = dot(in_ref[k, :, PIECE_COLS:], onehot)
        state = factor * state + in_ref[k, :, :PIECE_COLS].astype(F32)


def mix_kernel(x_ref, in_ref, map_ref, decay_ref, enter_ref, out_ref):
    cumulative = cumulative_of(decay_ref[...])
    middle = 0.5 * cumulative[T - 1 : T, :]
    onehot = head_spread()
    ahead = spread(jnp.exp(cumulative - middle), onehot)
    behind = spread(jnp.exp(middle - cumulative), onehot)
    start = spread(jnp.exp(jnp.broadcast_to(middle, (8, MIXER_HEADS))), onehot)[0:1, :]
    hi, lo = split2(x_ref[...].astype(F32) * behind)
    out_map = map_ref[...]
    match = dot_nt(out_map, in_ref[...])
    rows = lax.broadcasted_iota(jnp.int32, (T, T), 0)
    cols = lax.broadcasted_iota(jnp.int32, (T, T), 1)
    match_hi, match_lo = split2(jnp.where(cols <= rows, match, 0.0))
    inner = dot(match_hi, hi) + dot(match_hi, lo) + dot(match_lo, hi)
    for j in range(WIDTH // PIECE_COLS):
        cut = slice(j * PIECE_COLS, (j + 1) * PIECE_COLS)
        entering = jnp.concatenate(
            [enter_ref[i * (WIDTH // PIECE_COLS) + j] for i in range(N // PIECE_ROWS)], axis=0
        )
        carried = dot(out_map, entering)
        out_ref[:, cut] = (ahead[:, cut] * (inner[:, cut] + start[:, cut] * carried)).astype(BF16)


QUERIES = GROUP * T
KEYS = NH * T


def pack_kernel(k_ref, v_ref, after_ref, out_ref):
    for g in range(KVH):
        for i in range(NH):
            out_ref[i * NX + g, :DH, :] = k_ref[g * DH : (g + 1) * DH, :]
            out_ref[i * NX + g, DH:, :] = v_ref[g * DH : (g + 1) * DH, :]


def turn_kernel(place_ref, q_ref, *out_refs):
    for step, out_ref in enumerate(out_refs):
        g = lax.rem(place_ref[0] + step, NX)
        q = q_ref[:, pl.ds(pl.multiple_of(g * GDH, 128), GDH)].astype(F32)
        out_ref[...] = q.T.astype(BF16)


def scale_kernel(place_ref, *refs):
    scale = math.log2(math.e) / math.sqrt(DH)
    out_ref = refs[NX]
    blank = jnp.zeros((128 - DH, QUERIES), BF16)
    for s in range(NX):
        c = lax.rem(place_ref[0] + (NX - s), NX)
        out_ref[c, DH:128, :] = blank
        out_ref[c, 128 + DH :, :] = blank
        for h in range(GROUP):
            hi, lo = split2(refs[s][h * DH : (h + 1) * DH, :].astype(F32) * scale)
            out_ref[c, :DH, h * T : (h + 1) * T] = hi
            out_ref[c, 128 : 128 + DH, h * T : (h + 1) * T] = lo


def attend(place_ref, q_ref, block, parity, k_buf, v_buf, begin, end):
    z = place_ref[0]
    row = lax.broadcasted_iota(jnp.int32, (KEYS, QUERIES), 0)
    row = row + row // T * T + parity * T
    col = lax.broadcasted_iota(jnp.int32, (KEYS, QUERIES), 1) % T
    ones = jnp.where(lax.broadcasted_iota(jnp.int32, (16, KEYS), 0) == 0, 1.0, 0.0).astype(BF16)
    blank = jnp.zeros((128 - DH, T), F32)
    for c in range(NX):
        v_buf[DH:, c * KEYS : (c + 1) * KEYS] = ones
        for i in range(NH):
            at = slice(c * KEYS + i * T, c * KEYS + (i + 1) * T)
            kv = block(c, i)
            v_buf[:DH, at] = kv[DH:, :]
            k = jnp.concatenate([kv[:DH, :].astype(F32), blank], axis=0).T.astype(BF16)
            k_buf[at, :128] = k
            k_buf[at, 128:] = k
        q = q_ref[c]

        def scores(j, c=c, q=q):
            found = dot(k_buf[j * KEYS : (j + 1) * KEYS, :], q)
            if j == c:
                found = jnp.where(row <= col + z * T, found, masked_score)
            return found

        total, top = begin(c)
        found = scores(0)
        for j in range(c + 1):
            later = scores(j + 1) if j < c else None
            highest = jnp.max(found, axis=0, keepdims=True)
            if top is None:
                top = highest
            else:
                raised = jnp.maximum(top, highest)
                total = total * jnp.exp2(top - raised)
                top = raised
            expos = jnp.exp2(found - top).astype(BF16)
            summed = dot(v_buf[:, j * KEYS : (j + 1) * KEYS], expos)
            total = summed if total is None else total + summed
            found = later
        end(c, total, top)


def attend_same_kernel(place_ref, q_ref, same_ref, after_ref, total_ref, top_ref, *bufs):
    def end(c, total, top):
        total_ref[c] = total
        top_ref[c] = top

    attend(
        place_ref,
        q_ref,
        lambda c, i: same_ref[i * NX + c],
        place_ref[0] % 2,
        *bufs,
        lambda c: (None, None),
        end,
    )


def attend_other_kernel(
    place_ref, q_ref, below_ref, above_ref, total_ref, top_ref, out_ref, *bufs
):
    def end(c, total, top):
        done = (total[:DH, :] / total[DH : DH + 1, :]).astype(BF16)
        for h in range(GROUP):
            out_ref[c, h * DH : (h + 1) * DH, :] = done[:, h * T : (h + 1) * T]

    half = NH // 2
    attend(
        place_ref,
        q_ref,
        lambda c, i: (
            below_ref[i * NX + c] if i < half else above_ref[(i - half) * NX + c]
        ),
        1 - place_ref[0] % 2,
        *bufs,
        lambda c: (total_ref[c], top_ref[c]),
        end,
    )


def place_kernel(in_ref, after_ref, out_ref):
    for g in range(KVH):
        out_ref[:, g * GDH : (g + 1) * GDH] = in_ref[g].astype(F32).T.astype(BF16)


VMEM_SPEC = pl.BlockSpec(memory_space=pltpu.VMEM)
SMEM_SPEC = pl.BlockSpec(memory_space=pltpu.SMEM)
ANY_SPEC = pl.BlockSpec(memory_space=pl.ANY)


def call(kernel, shape, specs, scratch=(), limit=12):
    return pl.pallas_call(
        kernel,
        out_shape=jax.ShapeDtypeStruct(shape, BF16),
        in_specs=specs,
        out_specs=VMEM_SPEC,
        scratch_shapes=list(scratch),
        compiler_params=pltpu.CompilerParams(vmem_limit_bytes=limit << 20),
    )


def per_device(mixer_input, input_map, output_map, log_decay, query_rows, key_rows, value_rows):
    x = lax.axis_index("cx").astype(jnp.int32).reshape(1)
    z = lax.axis_index(("zh", "zl")).astype(jnp.int32).reshape(1)
    place = x * NZ + z
    turned = pl.pallas_call(
        turn_kernel,
        out_shape=[jax.ShapeDtypeStruct((GDH, T), BF16)] * NX,
        in_specs=[SMEM_SPEC, VMEM_SPEC],
        out_specs=[VMEM_SPEC] * NX,
        compiler_params=pltpu.CompilerParams(vmem_limit_bytes=12 << 20),
    )(x, query_rows)
    pack = call(pack_kernel, (NH * NX, 2 * DH, T), [VMEM_SPEC] * 2 + [ANY_SPEC])(
        key_rows.T, value_rows.T, turned[0]
    )
    same = lax.all_to_all(pack, ("zh", "cx"), 0, 0)
    half = NH * NX // 2
    below = lax.ppermute(same[:half], ("zh", "zl"), [(k, (k + 1) % NZ) for k in range(NZ)])
    above = lax.ppermute(same[half:], ("zh", "zl"), [(k, (k - 1) % NZ) for k in range(NZ)])
    turned = [turned[0]] + [
        lax.ppermute(turned[s], "cx", [(k, (k + s) % NX) for k in range(NX)])
        for s in range(1, NX)
    ]
    queries = call(scale_kernel, (NX, 256, QUERIES), [SMEM_SPEC] + [VMEM_SPEC] * NX)(x, *turned)
    update = call(
        update_kernel, (NCTX, PIECE_ROWS, PIECE_COLS + 128), [VMEM_SPEC] * 3
    )(mixer_input, input_map, log_decay.T)
    update = lax.all_to_all(update, ("cx", "zh", "zl"), 0, 0)
    prefix = call(prefix_kernel, (NCTX, PIECE_ROWS, PIECE_COLS), [SMEM_SPEC, VMEM_SPEC, ANY_SPEC])(
        place, update, queries
    )
    entering = lax.all_to_all(prefix, ("cx", "zh", "zl"), 0, 0)
    bufs = [
        pltpu.VMEM((NX * KEYS, 256), BF16),
        pltpu.VMEM((DH + 16, NX * KEYS), BF16),
    ]
    total, top = pl.pallas_call(
        attend_same_kernel,
        out_shape=[
            jax.ShapeDtypeStruct((NX, DH + 16, QUERIES), F32),
            jax.ShapeDtypeStruct((NX, 1, QUERIES), F32),
        ],
        in_specs=[SMEM_SPEC, VMEM_SPEC, VMEM_SPEC, ANY_SPEC],
        out_specs=[VMEM_SPEC, VMEM_SPEC],
        scratch_shapes=bufs,
        compiler_params=pltpu.CompilerParams(vmem_limit_bytes=24 << 20),
    )(z, queries, same, prefix)
    attended = call(
        attend_other_kernel, (NX, GDH, T), [SMEM_SPEC] + [VMEM_SPEC] * 5, bufs, 24
    )(z, queries, below, above, total, top)
    attended = lax.all_to_all(attended, "cx", 0, 0)
    mixer_output = call(mix_kernel, (T, WIDTH), [VMEM_SPEC] * 5)(
        mixer_input, input_map, output_map, log_decay.T, entering
    )
    attention_output = call(place_kernel, (T, QH * DH), [VMEM_SPEC, VMEM_SPEC])(
        attended, mixer_output[:16, :128]
    )
    return mixer_output, attention_output


def solution(mesh):
    grid = Mesh(mesh.devices.reshape(-1, NX, NH, 2), ("dp", "cx", "zh", "zl"))
    spec = P(("dp", "cx", "zh", "zl"), None)
    return jax.shard_map(
        per_device,
        mesh=grid,
        in_specs=(spec,) * 7,
        out_specs=(spec, spec),
        check_vma=False,
    )
```

```python
import math

import jax
import jax.numpy as jnp
from jax import lax
from jax.experimental import pallas as pl
from jax.experimental.pallas import tpu as pltpu
from jax.sharding import Mesh
from jax.sharding import PartitionSpec as P

MIXER_HEADS = 40
P_SIZE = 64
N = 128
QH = 32
KVH = 4
DH = 80
T = 128
WIDTH = MIXER_HEADS * P_SIZE
GROUP = QH // KVH
GDH = GROUP * DH
NX = 4
NH = 4
NZ = 2 * NH
NCTX = NX * NZ
PIECE_ROWS = 16
PIECE_COLS = 640
masked_score = -1e30
F32 = jnp.float32
BF16 = jnp.bfloat16


def split2(a):
    hi = a.astype(BF16)
    return hi, (a - hi.astype(F32)).astype(BF16)


def dot(a, b):
    return jnp.dot(a, b, preferred_element_type=F32)


def dot_nt(a, b):
    return lax.dot_general(a, b, (((1,), (1,)), ((), ())), preferred_element_type=F32)


def head_spread():
    rows = lax.broadcasted_iota(jnp.int32, (MIXER_HEADS, WIDTH), 0)
    cols = lax.broadcasted_iota(jnp.int32, (MIXER_HEADS, WIDTH), 1)
    return jnp.where(cols // P_SIZE == rows, 1.0, 0.0).astype(BF16)


def spread(a, onehot):
    hi, lo = split2(a)
    return dot(hi, onehot) + dot(lo, onehot)


def cumulative_of(decay):
    rows = lax.broadcasted_iota(jnp.int32, (T, T), 0)
    cols = lax.broadcasted_iota(jnp.int32, (T, T), 1)
    lower = jnp.where(cols <= rows, 1.0, 0.0).astype(F32)
    return lax.dot_general(
        lower,
        decay,
        (((1,), (1,)), ((), ())),
        precision=lax.Precision.HIGHEST,
        preferred_element_type=F32,
    )


def update_kernel(x_ref, in_ref, decay_ref, out_ref):
    cumulative = cumulative_of(decay_ref[...])
    last = cumulative[T - 1 : T, :]
    onehot = head_spread()
    tail = spread(jnp.exp(last - cumulative), onehot)
    hi, lo = split2(x_ref[...].astype(F32) * tail)
    in_t = in_ref[...].astype(F32).T.astype(BF16)
    update = (dot(in_t, hi) + dot(in_t, lo)).astype(BF16)
    total = jnp.broadcast_to(jnp.exp(last), (PIECE_ROWS, MIXER_HEADS))
    total_hi, total_lo = split2(total)
    head = lax.broadcasted_iota(jnp.int32, (MIXER_HEADS, 128), 0)
    lane = lax.broadcasted_iota(jnp.int32, (MIXER_HEADS, 128), 1)
    place_hi = jnp.where(lane == head, 1.0, 0.0).astype(BF16)
    place_lo = jnp.where(lane == head + 64, 1.0, 0.0).astype(BF16)
    factor = (dot(total_hi, place_hi) + dot(total_lo, place_lo)).astype(BF16)
    for i in range(N // PIECE_ROWS):
        for j in range(WIDTH // PIECE_COLS):
            d = i * (WIDTH // PIECE_COLS) + j
            out_ref[d, :, :PIECE_COLS] = update[
                i * PIECE_ROWS : (i + 1) * PIECE_ROWS, j * PIECE_COLS : (j + 1) * PIECE_COLS
            ]
            out_ref[d, :, PIECE_COLS:] = factor


def prefix_kernel(place_ref, in_ref, after_ref, below_ref, above_ref, out_ref):
    first_head = (place_ref[0] % (WIDTH // PIECE_COLS)) * (PIECE_COLS // P_SIZE)
    lane = lax.broadcasted_iota(jnp.int32, (128, PIECE_COLS), 0)
    cols = lax.broadcasted_iota(jnp.int32, (128, PIECE_COLS), 1)
    head = first_head + cols // P_SIZE
    onehot = jnp.where((lane == head) | (lane == head + 64), 1.0, 0.0).astype(BF16)
    state = jnp.zeros((PIECE_ROWS, PIECE_COLS), F32)
    for k in range(NCTX):
        out_ref[k] = state.astype(BF16)
        factor = dot(in_ref[k, :, PIECE_COLS:], onehot)
        state = factor * state + in_ref[k, :, :PIECE_COLS].astype(F32)


def mix_kernel(x_ref, in_ref, map_ref, decay_ref, enter_ref, out_ref, end_ref):
    end_ref[...] = jnp.zeros(end_ref.shape, F32)
    cumulative = cumulative_of(decay_ref[...])
    middle = 0.5 * cumulative[T - 1 : T, :]
    onehot = head_spread()
    ahead = spread(jnp.exp(cumulative - middle), onehot)
    behind = spread(jnp.exp(middle - cumulative), onehot)
    start = spread(jnp.exp(jnp.broadcast_to(middle, (8, MIXER_HEADS))), onehot)[0:1, :]
    hi, lo = split2(x_ref[...].astype(F32) * behind)
    out_map = map_ref[...]
    match = dot_nt(out_map, in_ref[...])
    rows = lax.broadcasted_iota(jnp.int32, (T, T), 0)
    cols = lax.broadcasted_iota(jnp.int32, (T, T), 1)
    match_hi, match_lo = split2(jnp.where(cols <= rows, match, 0.0))
    inner = dot(match_hi, hi) + dot(match_hi, lo) + dot(match_lo, hi)
    for j in range(WIDTH // PIECE_COLS):
        cut = slice(j * PIECE_COLS, (j + 1) * PIECE_COLS)
        entering = jnp.concatenate(
            [enter_ref[i * (WIDTH // PIECE_COLS) + j] for i in range(N // PIECE_ROWS)], axis=0
        )
        carried = dot(out_map, entering)
        out_ref[:, cut] = (ahead[:, cut] * (inner[:, cut] + start[:, cut] * carried)).astype(BF16)


QUERIES = GROUP * T
KEYS = NH * T


def pack_kernel(q_hbm, k_hbm, v_hbm, out_ref, q_ref, k_ref, v_ref, sems):
    copies = [
        pltpu.make_async_copy(q_hbm, q_ref, sems.at[0]),
        pltpu.make_async_copy(k_hbm, k_ref, sems.at[1]),
        pltpu.make_async_copy(v_hbm, v_ref, sems.at[2]),
    ]
    for copy in copies:
        copy.start()
    for copy in copies:
        copy.wait()
    for g in range(KVH):
        q = q_ref[:, g * GDH : (g + 1) * GDH].astype(F32)
        out_ref[g, :GDH, :] = q.T.astype(BF16)
        out_ref[g, GDH : GDH + DH, :] = k_ref[g * DH : (g + 1) * DH, :]
        out_ref[g, GDH + DH :, :] = v_ref[g * DH : (g + 1) * DH, :]


def attend(place_ref, q_ref, block, parity, k_buf, v_buf, q_buf, begin, end):
    z = place_ref[0]
    scale = math.log2(math.e) / math.sqrt(DH)
    row = lax.broadcasted_iota(jnp.int32, (KEYS, QUERIES), 0)
    row = row + row // T * T + parity * T
    col = lax.broadcasted_iota(jnp.int32, (KEYS, QUERIES), 1) % T
    ones = jnp.where(lax.broadcasted_iota(jnp.int32, (16, KEYS), 0) == 0, 1.0, 0.0).astype(BF16)
    blank = jnp.zeros((128 - DH, T), F32)
    blank_q = jnp.zeros((128 - DH, QUERIES), BF16)
    for c in range(NX):
        q_buf[DH:128, :] = blank_q
        q_buf[128 + DH :, :] = blank_q
        for h in range(GROUP):
            hi, lo = split2(q_ref[c, h * DH : (h + 1) * DH, :].astype(F32) * scale)
            q_buf[:DH, h * T : (h + 1) * T] = hi
            q_buf[128 : 128 + DH, h * T : (h + 1) * T] = lo
        v_buf[DH:, c * KEYS : (c + 1) * KEYS] = ones
        for i in range(NH):
            at = slice(c * KEYS + i * T, c * KEYS + (i + 1) * T)
            kv = block(c, i)
            v_buf[:DH, at] = kv[DH:, :]
            k = jnp.concatenate([kv[:DH, :].astype(F32), blank], axis=0).T.astype(BF16)
            k_buf[at, :128] = k
            k_buf[at, 128:] = k
        q = q_buf[...]

        def scores(j, c=c, q=q):
            found = dot(k_buf[j * KEYS : (j + 1) * KEYS, :], q)
            if j == c:
                found = jnp.where(row <= col + z * T, found, masked_score)
            return found

        total, top = begin(c)
        found = scores(0)
        for j in range(c + 1):
            later = scores(j + 1) if j < c else None
            highest = jnp.max(found, axis=0, keepdims=True)
            if top is None:
                top = highest
            else:
                raised = jnp.maximum(top, highest)
                total = total * jnp.exp2(top - raised)
                top = raised
            expos = jnp.exp2(found - top).astype(BF16)
            summed = dot(v_buf[:, j * KEYS : (j + 1) * KEYS], expos)
            total = summed if total is None else total + summed
            found = later
        end(c, total, top)


def attend_same_kernel(place_ref, q_ref, same_ref, total_ref, top_ref, *bufs):
    def end(c, total, top):
        total_ref[c] = total
        top_ref[c] = top

    attend(
        place_ref,
        q_ref,
        lambda c, i: same_ref[i, c],
        place_ref[0] % 2,
        *bufs,
        lambda c: (None, None),
        end,
    )


def attend_other_kernel(
    place_ref, q_ref, below_ref, above_ref, total_ref, top_ref, after_ref, out_ref, *bufs
):
    def end(c, total, top):
        done = (total[:DH, :] / total[DH : DH + 1, :]).astype(BF16)
        for h in range(GROUP):
            out_ref[c, h * DH : (h + 1) * DH, :] = done[:, h * T : (h + 1) * T]

    half = NH // 2
    attend(
        place_ref,
        q_ref,
        lambda c, i: below_ref[i, c] if i < half else above_ref[i - half, c],
        1 - place_ref[0] % 2,
        *bufs,
        lambda c: (total_ref[c], top_ref[c]),
        end,
    )


def place_kernel(in_ref, after_ref, out_ref):
    for g in range(KVH):
        out_ref[:, g * GDH : (g + 1) * GDH] = in_ref[g].astype(F32).T.astype(BF16)


PACK_BUFS = [
    pltpu.VMEM((T, QH * DH), BF16),
    pltpu.VMEM((KVH * DH, T), BF16),
    pltpu.VMEM((KVH * DH, T), BF16),
    pltpu.SemaphoreType.DMA((3,)),
]
VMEM_SPEC = pl.BlockSpec(memory_space=pltpu.VMEM)
SMEM_SPEC = pl.BlockSpec(memory_space=pltpu.SMEM)
ANY_SPEC = pl.BlockSpec(memory_space=pl.ANY)


def call(kernel, shape, specs, scratch=(), limit=12):
    return pl.pallas_call(
        kernel,
        out_shape=jax.ShapeDtypeStruct(shape, BF16),
        in_specs=specs,
        out_specs=VMEM_SPEC,
        scratch_shapes=list(scratch),
        compiler_params=pltpu.CompilerParams(vmem_limit_bytes=limit << 20),
    )


def per_device(mixer_input, input_map, output_map, log_decay, query_rows, key_rows, value_rows):
    place_z = lax.axis_index(("zh", "zl")).astype(jnp.int32).reshape(1)
    place = lax.axis_index(("cx", "zh", "zl")).astype(jnp.int32).reshape(1)
    packed = call(pack_kernel, (KVH, GDH + 2 * DH, T), [ANY_SPEC] * 3, PACK_BUFS)(
        query_rows, key_rows.T, value_rows.T
    )
    packed = lax.all_to_all(packed, "cx", 0, 0)
    kv = packed[:, GDH:, :]
    same = lax.all_to_all(jnp.broadcast_to(kv[None], (NH,) + kv.shape), "zh", 0, 0)
    below = lax.ppermute(same[: NH // 2], ("zh", "zl"), [(k, (k + 1) % NZ) for k in range(NZ)])
    above = lax.ppermute(same[NH // 2 :], ("zh", "zl"), [(k, (k - 1) % NZ) for k in range(NZ)])
    update = call(
        update_kernel, (NCTX, PIECE_ROWS, PIECE_COLS + 128), [VMEM_SPEC] * 3
    )(mixer_input, input_map, log_decay.T)
    update = lax.all_to_all(update, ("cx", "zh", "zl"), 0, 0)
    bufs = [
        pltpu.VMEM((NX * KEYS, 256), BF16),
        pltpu.VMEM((DH + 16, NX * KEYS), BF16),
        pltpu.VMEM((256, QUERIES), BF16),
    ]
    total, top = pl.pallas_call(
        attend_same_kernel,
        out_shape=[
            jax.ShapeDtypeStruct((NX, DH + 16, QUERIES), F32),
            jax.ShapeDtypeStruct((NX, 1, QUERIES), F32),
        ],
        in_specs=[SMEM_SPEC, VMEM_SPEC, VMEM_SPEC],
        out_specs=[VMEM_SPEC, VMEM_SPEC],
        scratch_shapes=bufs,
        compiler_params=pltpu.CompilerParams(vmem_limit_bytes=24 << 20),
    )(place_z, packed, same)
    prefix = call(
        prefix_kernel,
        (NCTX, PIECE_ROWS, PIECE_COLS),
        [SMEM_SPEC, VMEM_SPEC, VMEM_SPEC, ANY_SPEC, ANY_SPEC],
    )(place, update, top, below, above)
    entering = lax.all_to_all(prefix, ("cx", "zh", "zl"), 0, 0)
    attended = call(
        attend_other_kernel, (NX, GDH, T), [SMEM_SPEC] + [VMEM_SPEC] * 5 + [ANY_SPEC], bufs, 24
    )(place_z, packed, below, above, total, top, prefix)
    attended = lax.all_to_all(attended, "cx", 0, 0)
    mixer_output, end = pl.pallas_call(
        mix_kernel,
        out_shape=[
            jax.ShapeDtypeStruct((T, WIDTH), BF16),
            jax.ShapeDtypeStruct((8, 128), F32),
        ],
        in_specs=[VMEM_SPEC] * 5,
        out_specs=[VMEM_SPEC] * 2,
        compiler_params=pltpu.CompilerParams(vmem_limit_bytes=12 << 20),
    )(mixer_input, input_map, output_map, log_decay.T, entering)
    attention_output = call(place_kernel, (T, QH * DH), [VMEM_SPEC, VMEM_SPEC])(attended, end)
    return mixer_output, attention_output


def solution(mesh):
    grid = Mesh(mesh.devices.reshape(-1, NX, NH, 2), ("dp", "cx", "zh", "zl"))
    spec = P(("dp", "cx", "zh", "zl"), None)
    return jax.shard_map(
        per_device,
        mesh=grid,
        in_specs=(spec,) * 7,
        out_specs=(spec, spec),
        check_vma=False,
    )
```

```python
import math

import jax
import jax.numpy as jnp
from jax import lax
from jax.experimental import pallas as pl
from jax.experimental.pallas import tpu as pltpu
from jax.sharding import Mesh
from jax.sharding import PartitionSpec as P

MIXER_HEADS = 40
P_SIZE = 64
N = 128
QH = 32
KVH = 4
DH = 80
T = 128
WIDTH = MIXER_HEADS * P_SIZE
GROUP = QH // KVH
GDH = GROUP * DH
NX = 4
NH = 4
NZ = 2 * NH
NCTX = NX * NZ
PIECE_ROWS = 16
PIECE_COLS = 640
masked_score = -1e30
F32 = jnp.float32
BF16 = jnp.bfloat16


def split2(a):
    hi = a.astype(BF16)
    return hi, (a - hi.astype(F32)).astype(BF16)


def dot(a, b):
    return jnp.dot(a, b, preferred_element_type=F32)


def dot_nt(a, b):
    return lax.dot_general(a, b, (((1,), (1,)), ((), ())), preferred_element_type=F32)


def head_spread():
    rows = lax.broadcasted_iota(jnp.int32, (MIXER_HEADS, WIDTH), 0)
    cols = lax.broadcasted_iota(jnp.int32, (MIXER_HEADS, WIDTH), 1)
    return jnp.where(cols // P_SIZE == rows, 1.0, 0.0).astype(BF16)


def spread(a, onehot):
    hi, lo = split2(a)
    return dot(hi, onehot) + dot(lo, onehot)


def cumulative_of(decay):
    rows = lax.broadcasted_iota(jnp.int32, (T, T), 0)
    cols = lax.broadcasted_iota(jnp.int32, (T, T), 1)
    lower = jnp.where(cols <= rows, 1.0, 0.0).astype(F32)
    return lax.dot_general(
        lower,
        decay,
        (((1,), (1,)), ((), ())),
        precision=lax.Precision.HIGHEST,
        preferred_element_type=F32,
    )


def update_kernel(x_ref, in_ref, decay_ref, out_ref):
    cumulative = cumulative_of(decay_ref[...])
    last = cumulative[T - 1 : T, :]
    tail = spread(jnp.exp(last - cumulative), head_spread())
    hi, lo = split2(x_ref[...].astype(F32) * tail)
    in_t = in_ref[...].astype(F32).T.astype(BF16)
    out_ref[...] = (dot(in_t, hi) + dot(in_t, lo)).astype(BF16)


def cut_kernel(in_ref, after_ref, out_ref):
    across = WIDTH // PIECE_COLS
    for i in range(N // PIECE_ROWS):
        for j in range(across):
            out_ref[i * across + j] = in_ref[
                i * PIECE_ROWS : (i + 1) * PIECE_ROWS, j * PIECE_COLS : (j + 1) * PIECE_COLS
            ]


def prefix_kernel(place_ref, in_ref, same_ref, below_ref, above_ref, after_ref, out_ref):
    first_head = (place_ref[0] % (WIDTH // PIECE_COLS)) * (PIECE_COLS // P_SIZE)
    parity = place_ref[0] % 2
    lane = lax.broadcasted_iota(jnp.int32, (128, PIECE_COLS), 0)
    cols = lax.broadcasted_iota(jnp.int32, (128, PIECE_COLS), 1)
    head = first_head + cols // P_SIZE
    onehot = jnp.where((lane == head) | (lane == head + 64), 1.0, 0.0).astype(BF16)
    state = jnp.zeros((PIECE_ROWS, PIECE_COLS), F32)
    half = NH // 2
    for k in range(NCTX):
        out_ref[k] = state.astype(BF16)
        c, i = k // NZ, k % NZ // 2
        mine = same_ref[i, c, 2 * DH :, :].astype(F32)
        other = below_ref[i, c, 2 * DH :, :] if i < half else above_ref[i - half, c, 2 * DH :, :]
        decay = jnp.where(parity == k % 2, mine, other.astype(F32)).astype(BF16)
        state = dot(decay, onehot) * state + in_ref[k].astype(F32)


def mix_kernel(x_ref, in_ref, map_ref, decay_ref, enter_ref, out_ref, end_ref):
    end_ref[...] = jnp.zeros(end_ref.shape, F32)
    cumulative = cumulative_of(decay_ref[...])
    middle = 0.5 * cumulative[T - 1 : T, :]
    onehot = head_spread()
    ahead = spread(jnp.exp(cumulative - middle), onehot)
    behind = spread(jnp.exp(middle - cumulative), onehot)
    start = spread(jnp.exp(jnp.broadcast_to(middle, (8, MIXER_HEADS))), onehot)[0:1, :]
    hi, lo = split2(x_ref[...].astype(F32) * behind)
    out_map = map_ref[...]
    match = dot_nt(out_map, in_ref[...])
    rows = lax.broadcasted_iota(jnp.int32, (T, T), 0)
    cols = lax.broadcasted_iota(jnp.int32, (T, T), 1)
    match_hi, match_lo = split2(jnp.where(cols <= rows, match, 0.0))
    inner = dot(match_hi, hi) + dot(match_hi, lo) + dot(match_lo, hi)
    for j in range(WIDTH // PIECE_COLS):
        cut = slice(j * PIECE_COLS, (j + 1) * PIECE_COLS)
        entering = jnp.concatenate(
            [enter_ref[i * (WIDTH // PIECE_COLS) + j] for i in range(N // PIECE_ROWS)], axis=0
        )
        carried = dot(out_map, entering)
        out_ref[:, cut] = (ahead[:, cut] * (inner[:, cut] + start[:, cut] * carried)).astype(BF16)


QUERIES = GROUP * T
KEYS = NH * T


def pack_kernel(q_ref, k_ref, v_ref, decay_ref, out_ref):
    total = lax.dot_general(
        jnp.ones((PIECE_ROWS, T), F32),
        decay_ref[...],
        (((1,), (1,)), ((), ())),
        precision=lax.Precision.HIGHEST,
        preferred_element_type=F32,
    )
    total_hi, total_lo = split2(jnp.exp(total))
    head = lax.broadcasted_iota(jnp.int32, (MIXER_HEADS, 128), 0)
    lane = lax.broadcasted_iota(jnp.int32, (MIXER_HEADS, 128), 1)
    place_hi = jnp.where(lane == head, 1.0, 0.0).astype(BF16)
    place_lo = jnp.where(lane == head + 64, 1.0, 0.0).astype(BF16)
    decay = (dot(total_hi, place_hi) + dot(total_lo, place_lo)).astype(BF16)
    for g in range(KVH):
        q = q_ref[:, g * GDH : (g + 1) * GDH].astype(F32)
        out_ref[g, :GDH, :] = q.T.astype(BF16)
        out_ref[g, GDH : GDH + DH, :] = k_ref[g * DH : (g + 1) * DH, :]
        out_ref[g, GDH + DH : GDH + 2 * DH, :] = v_ref[g * DH : (g + 1) * DH, :]
        out_ref[g, GDH + 2 * DH :, :] = decay


def attend(place_ref, q_ref, block, parity, k_buf, v_buf, q_buf, begin, end):
    z = place_ref[0]
    scale = math.log2(math.e) / math.sqrt(DH)
    row = lax.broadcasted_iota(jnp.int32, (KEYS, QUERIES), 0)
    row = row + row // T * T + parity * T
    col = lax.broadcasted_iota(jnp.int32, (KEYS, QUERIES), 1) % T
    ones = jnp.where(lax.broadcasted_iota(jnp.int32, (16, KEYS), 0) == 0, 1.0, 0.0).astype(BF16)
    blank = jnp.zeros((128 - DH, T), F32)
    blank_q = jnp.zeros((128 - DH, QUERIES), BF16)
    for c in range(NX):
        q_buf[DH:128, :] = blank_q
        q_buf[128 + DH :, :] = blank_q
        for h in range(GROUP):
            hi, lo = split2(q_ref[c, h * DH : (h + 1) * DH, :].astype(F32) * scale)
            q_buf[:DH, h * T : (h + 1) * T] = hi
            q_buf[128 : 128 + DH, h * T : (h + 1) * T] = lo
        v_buf[DH:, c * KEYS : (c + 1) * KEYS] = ones
        for i in range(NH):
            at = slice(c * KEYS + i * T, c * KEYS + (i + 1) * T)
            kv = block(c, i)
            v_buf[:DH, at] = kv[DH : 2 * DH, :]
            k = jnp.concatenate([kv[:DH, :].astype(F32), blank], axis=0).T.astype(BF16)
            k_buf[at, :128] = k
            k_buf[at, 128:] = k
        q = q_buf[...]

        def scores(j, c=c, q=q):
            found = dot(k_buf[j * KEYS : (j + 1) * KEYS, :], q)
            if j == c:
                found = jnp.where(row <= col + z * T, found, masked_score)
            return found

        total, top = begin(c)
        found = scores(0)
        for j in range(c + 1):
            later = scores(j + 1) if j < c else None
            highest = jnp.max(found, axis=0, keepdims=True)
            if top is None:
                top = highest
            else:
                raised = jnp.maximum(top, highest)
                total = total * jnp.exp2(top - raised)
                top = raised
            expos = jnp.exp2(found - top).astype(BF16)
            summed = dot(v_buf[:, j * KEYS : (j + 1) * KEYS], expos)
            total = summed if total is None else total + summed
            found = later
        end(c, total, top)


def attend_same_kernel(place_ref, q_ref, same_ref, total_ref, top_ref, *bufs):
    def end(c, total, top):
        total_ref[c] = total
        top_ref[c] = top

    attend(
        place_ref,
        q_ref,
        lambda c, i: same_ref[i, c],
        place_ref[0] % 2,
        *bufs,
        lambda c: (None, None),
        end,
    )


def attend_other_kernel(
    place_ref, q_ref, below_ref, above_ref, total_ref, top_ref, after_ref, out_ref, *bufs
):
    def end(c, total, top):
        done = (total[:DH, :] / total[DH : DH + 1, :]).astype(BF16)
        for h in range(GROUP):
            out_ref[c, h * DH : (h + 1) * DH, :] = done[:, h * T : (h + 1) * T]

    half = NH // 2
    attend(
        place_ref,
        q_ref,
        lambda c, i: below_ref[i, c] if i < half else above_ref[i - half, c],
        1 - place_ref[0] % 2,
        *bufs,
        lambda c: (total_ref[c], top_ref[c]),
        end,
    )


def place_kernel(in_ref, after_ref, out_ref):
    for g in range(KVH):
        out_ref[:, g * GDH : (g + 1) * GDH] = in_ref[g].astype(F32).T.astype(BF16)


VMEM_SPEC = pl.BlockSpec(memory_space=pltpu.VMEM)
SMEM_SPEC = pl.BlockSpec(memory_space=pltpu.SMEM)
ANY_SPEC = pl.BlockSpec(memory_space=pl.ANY)


def call(kernel, shape, specs, scratch=(), limit=12):
    return pl.pallas_call(
        kernel,
        out_shape=jax.ShapeDtypeStruct(shape, BF16),
        in_specs=specs,
        out_specs=VMEM_SPEC,
        scratch_shapes=list(scratch),
        compiler_params=pltpu.CompilerParams(vmem_limit_bytes=limit << 20),
    )


def per_device(mixer_input, input_map, output_map, log_decay, query_rows, key_rows, value_rows):
    place_z = lax.axis_index(("zh", "zl")).astype(jnp.int32).reshape(1)
    place = lax.axis_index(("cx", "zh", "zl")).astype(jnp.int32).reshape(1)
    packed = call(pack_kernel, (KVH, GDH + 2 * DH + PIECE_ROWS, T), [VMEM_SPEC] * 4)(
        query_rows, key_rows.T, value_rows.T, log_decay.T
    )
    packed = lax.all_to_all(packed, "cx", 0, 0)
    same = lax.all_gather(packed[:, GDH:, :], "zh")
    below = lax.ppermute(same[: NH // 2], ("zh", "zl"), [(k, (k + 1) % NZ) for k in range(NZ)])
    above = lax.ppermute(same[NH // 2 :], ("zh", "zl"), [(k, (k - 1) % NZ) for k in range(NZ)])
    update = call(update_kernel, (N, WIDTH), [VMEM_SPEC] * 3)(
        mixer_input, input_map, log_decay.T
    )
    update = call(cut_kernel, (NCTX, PIECE_ROWS, PIECE_COLS), [VMEM_SPEC, ANY_SPEC])(update, same)
    update = lax.all_to_all(update, ("cx", "zh", "zl"), 0, 0)
    bufs = [
        pltpu.VMEM((NX * KEYS, 256), BF16),
        pltpu.VMEM((DH + 16, NX * KEYS), BF16),
        pltpu.VMEM((256, QUERIES), BF16),
    ]
    total, top = pl.pallas_call(
        attend_same_kernel,
        out_shape=[
            jax.ShapeDtypeStruct((NX, DH + 16, QUERIES), F32),
            jax.ShapeDtypeStruct((NX, 1, QUERIES), F32),
        ],
        in_specs=[SMEM_SPEC, VMEM_SPEC, VMEM_SPEC],
        out_specs=[VMEM_SPEC, VMEM_SPEC],
        scratch_shapes=bufs,
        compiler_params=pltpu.CompilerParams(vmem_limit_bytes=24 << 20),
    )(place_z, packed, same)
    prefix = call(prefix_kernel, (NCTX, PIECE_ROWS, PIECE_COLS), [SMEM_SPEC] + [VMEM_SPEC] * 5)(
        place, update, same, below, above, top
    )
    entering = lax.all_to_all(prefix, ("cx", "zh", "zl"), 0, 0)
    attended = call(
        attend_other_kernel, (NX, GDH, T), [SMEM_SPEC] + [VMEM_SPEC] * 5 + [ANY_SPEC], bufs, 24
    )(place_z, packed, below, above, total, top, prefix)
    attended = lax.all_to_all(attended, "cx", 0, 0)
    mixer_output, end = pl.pallas_call(
        mix_kernel,
        out_shape=[
            jax.ShapeDtypeStruct((T, WIDTH), BF16),
            jax.ShapeDtypeStruct((8, 128), F32),
        ],
        in_specs=[VMEM_SPEC] * 5,
        out_specs=[VMEM_SPEC] * 2,
        compiler_params=pltpu.CompilerParams(vmem_limit_bytes=12 << 20),
    )(mixer_input, input_map, output_map, log_decay.T, entering)
    attention_output = call(place_kernel, (T, QH * DH), [VMEM_SPEC, VMEM_SPEC])(attended, end)
    return mixer_output, attention_output


def solution(mesh):
    grid = Mesh(mesh.devices.reshape(-1, NX, NH, 2), ("dp", "cx", "zh", "zl"))
    spec = P(("dp", "cx", "zh", "zl"), None)
    return jax.shard_map(
        per_device,
        mesh=grid,
        in_specs=(spec,) * 7,
        out_specs=(spec, spec),
        check_vma=False,
    )
```

```python
import math

import jax
import jax.numpy as jnp
from jax import lax
from jax.experimental import pallas as pl
from jax.experimental.pallas import tpu as pltpu
from jax.sharding import Mesh
from jax.sharding import PartitionSpec as P

MIXER_HEADS = 40
P_SIZE = 64
N = 128
QH = 32
KVH = 4
DH = 80
T = 128
WIDTH = MIXER_HEADS * P_SIZE
GROUP = QH // KVH
GDH = GROUP * DH
NX = 4
NH = 4
NZ = 2 * NH
NCTX = NX * NZ
PIECE_ROWS = 16
PIECE_COLS = 640
masked_score = -1e30
F32 = jnp.float32
BF16 = jnp.bfloat16


def split2(a):
    hi = a.astype(BF16)
    return hi, (a - hi.astype(F32)).astype(BF16)


def dot(a, b):
    return jnp.dot(a, b, preferred_element_type=F32)


def dot_nt(a, b):
    return lax.dot_general(a, b, (((1,), (1,)), ((), ())), preferred_element_type=F32)


def head_spread():
    rows = lax.broadcasted_iota(jnp.int32, (MIXER_HEADS, WIDTH), 0)
    cols = lax.broadcasted_iota(jnp.int32, (MIXER_HEADS, WIDTH), 1)
    return jnp.where(cols // P_SIZE == rows, 1.0, 0.0).astype(BF16)


def spread(a, onehot):
    hi, lo = split2(a)
    return dot(hi, onehot) + dot(lo, onehot)


def cumulative_of(decay):
    rows = lax.broadcasted_iota(jnp.int32, (T, T), 0)
    cols = lax.broadcasted_iota(jnp.int32, (T, T), 1)
    lower = jnp.where(cols <= rows, 1.0, 0.0).astype(F32)
    return lax.dot_general(
        lower,
        decay,
        (((1,), (1,)), ((), ())),
        precision=lax.Precision.HIGHEST,
        preferred_element_type=F32,
    )


def update_kernel(x_ref, in_ref, decay_ref, out_ref):
    cumulative = cumulative_of(decay_ref[...])
    last = cumulative[T - 1 : T, :]
    tail = spread(jnp.exp(last - cumulative), head_spread())
    hi, lo = split2(x_ref[...].astype(F32) * tail)
    in_t = in_ref[...].astype(F32).T.astype(BF16)
    out_ref[...] = (dot(in_t, hi) + dot(in_t, lo)).astype(BF16)


def cut_kernel(in_ref, after_ref, out_ref):
    across = WIDTH // PIECE_COLS
    for i in range(N // PIECE_ROWS):
        for j in range(across):
            out_ref[i * across + j] = in_ref[
                i * PIECE_ROWS : (i + 1) * PIECE_ROWS, j * PIECE_COLS : (j + 1) * PIECE_COLS
            ]


def prefix_kernel(place_ref, in_ref, same_ref, below_ref, above_ref, after_ref, out_ref):
    first_head = (place_ref[0] % (WIDTH // PIECE_COLS)) * (PIECE_COLS // P_SIZE)
    parity = place_ref[0] % 2
    lane = lax.broadcasted_iota(jnp.int32, (128, PIECE_COLS), 0)
    cols = lax.broadcasted_iota(jnp.int32, (128, PIECE_COLS), 1)
    head = first_head + cols // P_SIZE
    onehot = jnp.where((lane == head) | (lane == head + 64), 1.0, 0.0).astype(BF16)
    state = jnp.zeros((PIECE_ROWS, PIECE_COLS), F32)
    half = NH // 2
    for k in range(NCTX):
        out_ref[k] = state.astype(BF16)
        c, i = k // NZ, k % NZ // 2
        mine = same_ref[i, c, 2 * DH :, :].astype(F32)
        other = below_ref[i, c, 2 * DH :, :] if i < half else above_ref[i - half, c, 2 * DH :, :]
        decay = jnp.where(parity == k % 2, mine, other.astype(F32)).astype(BF16)
        state = dot(decay, onehot) * state + in_ref[k].astype(F32)


def mix_kernel(x_ref, in_ref, map_ref, decay_ref, enter_ref, out_ref, end_ref):
    end_ref[...] = jnp.zeros(end_ref.shape, F32)
    cumulative = cumulative_of(decay_ref[...])
    middle = 0.5 * cumulative[T - 1 : T, :]
    onehot = head_spread()
    ahead = spread(jnp.exp(cumulative - middle), onehot)
    behind = spread(jnp.exp(middle - cumulative), onehot)
    start = spread(jnp.exp(jnp.broadcast_to(middle, (8, MIXER_HEADS))), onehot)[0:1, :]
    hi, lo = split2(x_ref[...].astype(F32) * behind)
    out_map = map_ref[...]
    match = dot_nt(out_map, in_ref[...])
    rows = lax.broadcasted_iota(jnp.int32, (T, T), 0)
    cols = lax.broadcasted_iota(jnp.int32, (T, T), 1)
    match_hi, match_lo = split2(jnp.where(cols <= rows, match, 0.0))
    inner = dot(match_hi, hi) + dot(match_hi, lo) + dot(match_lo, hi)
    for j in range(WIDTH // PIECE_COLS):
        cut = slice(j * PIECE_COLS, (j + 1) * PIECE_COLS)
        entering = jnp.concatenate(
            [enter_ref[i * (WIDTH // PIECE_COLS) + j] for i in range(N // PIECE_ROWS)], axis=0
        )
        carried = dot(out_map, entering)
        out_ref[:, cut] = (ahead[:, cut] * (inner[:, cut] + start[:, cut] * carried)).astype(BF16)


QUERIES = GROUP * T
KEYS = NH * T


def pack_kernel(q_ref, k_ref, v_ref, decay_ref, out_ref):
    total = lax.dot_general(
        jnp.ones((PIECE_ROWS, T), F32),
        decay_ref[...],
        (((1,), (1,)), ((), ())),
        precision=lax.Precision.HIGHEST,
        preferred_element_type=F32,
    )
    total_hi, total_lo = split2(jnp.exp(total))
    head = lax.broadcasted_iota(jnp.int32, (MIXER_HEADS, 128), 0)
    lane = lax.broadcasted_iota(jnp.int32, (MIXER_HEADS, 128), 1)
    place_hi = jnp.where(lane == head, 1.0, 0.0).astype(BF16)
    place_lo = jnp.where(lane == head + 64, 1.0, 0.0).astype(BF16)
    decay = (dot(total_hi, place_hi) + dot(total_lo, place_lo)).astype(BF16)
    for g in range(KVH):
        q = q_ref[:, g * GDH : (g + 1) * GDH].astype(F32)
        out_ref[g, :GDH, :] = q.T.astype(BF16)
        out_ref[g, GDH : GDH + DH, :] = k_ref[g * DH : (g + 1) * DH, :]
        out_ref[g, GDH + DH : GDH + 2 * DH, :] = v_ref[g * DH : (g + 1) * DH, :]
        out_ref[g, GDH + 2 * DH :, :] = decay


def attend(place_ref, q_ref, block, parity, k_buf, v_buf, q_buf, begin, end):
    z = place_ref[0]
    scale = math.log2(math.e) / math.sqrt(DH)
    row = lax.broadcasted_iota(jnp.int32, (KEYS, QUERIES), 0)
    row = row + row // T * T + parity * T
    col = lax.broadcasted_iota(jnp.int32, (KEYS, QUERIES), 1) % T
    ones = jnp.where(lax.broadcasted_iota(jnp.int32, (16, KEYS), 0) == 0, 1.0, 0.0).astype(BF16)
    blank = jnp.zeros((128 - DH, T), F32)
    blank_q = jnp.zeros((128 - DH, QUERIES), BF16)
    for c in range(NX):
        q_buf[DH:128, :] = blank_q
        q_buf[128 + DH :, :] = blank_q
        for h in range(GROUP):
            hi, lo = split2(q_ref[c, h * DH : (h + 1) * DH, :].astype(F32) * scale)
            q_buf[:DH, h * T : (h + 1) * T] = hi
            q_buf[128 : 128 + DH, h * T : (h + 1) * T] = lo
        v_buf[DH:, c * KEYS : (c + 1) * KEYS] = ones
        for i in range(NH):
            at = slice(c * KEYS + i * T, c * KEYS + (i + 1) * T)
            kv = block(c, i)
            v_buf[:DH, at] = kv[DH : 2 * DH, :]
            k = jnp.concatenate([kv[:DH, :].astype(F32), blank], axis=0).T.astype(BF16)
            k_buf[at, :128] = k
            k_buf[at, 128:] = k
        q = q_buf[...]

        def scores(j, c=c, q=q):
            found = dot(k_buf[j * KEYS : (j + 1) * KEYS, :], q)
            if j == c:
                found = jnp.where(row <= col + z * T, found, masked_score)
            return found

        total, top = begin(c)
        found = scores(0)
        for j in range(c + 1):
            later = scores(j + 1) if j < c else None
            highest = jnp.max(found, axis=0, keepdims=True)
            if top is None:
                top = highest
            else:
                raised = jnp.maximum(top, highest)
                total = total * jnp.exp2(top - raised)
                top = raised
            expos = jnp.exp2(found - top).astype(BF16)
            summed = dot(v_buf[:, j * KEYS : (j + 1) * KEYS], expos)
            total = summed if total is None else total + summed
            found = later
        end(c, total, top)


def attend_same_kernel(place_ref, q_ref, same_ref, total_ref, top_ref, *bufs):
    def end(c, total, top):
        total_ref[c] = total
        top_ref[c] = top

    attend(
        place_ref,
        q_ref,
        lambda c, i: same_ref[i, c],
        place_ref[0] % 2,
        *bufs,
        lambda c: (None, None),
        end,
    )


def attend_other_kernel(
    place_ref, q_ref, below_ref, above_ref, total_ref, top_ref, after_ref, *refs
):
    out_refs, bufs = refs[:NX], refs[NX:]

    def end(c, total, top):
        done = (total[:DH, :] / total[DH : DH + 1, :]).astype(BF16)
        step = lax.rem(c + NX - place_ref[1], NX)
        for s in range(NX):

            @pl.when(step == s)
            def _(out_ref=out_refs[s]):
                for h in range(GROUP):
                    out_ref[h * DH : (h + 1) * DH, :] = done[:, h * T : (h + 1) * T]

    half = NH // 2
    attend(
        place_ref,
        q_ref,
        lambda c, i: below_ref[i, c] if i < half else above_ref[i - half, c],
        1 - place_ref[0] % 2,
        *bufs,
        lambda c: (total_ref[c], top_ref[c]),
        end,
    )


def place_kernel(place_ref, *refs):
    out_ref = refs[-1]
    for s in range(NX):
        g = lax.rem(place_ref[1] + (NX - s), NX)
        cols = pl.ds(pl.multiple_of(g * GDH, 128), GDH)
        out_ref[:, cols] = refs[s][...].astype(F32).T.astype(BF16)


VMEM_SPEC = pl.BlockSpec(memory_space=pltpu.VMEM)
SMEM_SPEC = pl.BlockSpec(memory_space=pltpu.SMEM)
ANY_SPEC = pl.BlockSpec(memory_space=pl.ANY)


def call(kernel, shape, specs, scratch=(), limit=12):
    return pl.pallas_call(
        kernel,
        out_shape=jax.ShapeDtypeStruct(shape, BF16),
        in_specs=specs,
        out_specs=VMEM_SPEC,
        scratch_shapes=list(scratch),
        compiler_params=pltpu.CompilerParams(vmem_limit_bytes=limit << 20),
    )


def per_device(mixer_input, input_map, output_map, log_decay, query_rows, key_rows, value_rows):
    place_zx = jnp.stack([lax.axis_index(("zh", "zl")), lax.axis_index("cx")]).astype(jnp.int32)
    place = lax.axis_index(("cx", "zh", "zl")).astype(jnp.int32).reshape(1)
    packed = call(pack_kernel, (KVH, GDH + 2 * DH + PIECE_ROWS, T), [VMEM_SPEC] * 4)(
        query_rows, key_rows.T, value_rows.T, log_decay.T
    )
    packed = lax.all_to_all(packed, "cx", 0, 0)
    same = lax.all_gather(packed[:, GDH:, :], "zh")
    below = lax.ppermute(same[: NH // 2], ("zh", "zl"), [(k, (k + 1) % NZ) for k in range(NZ)])
    above = lax.ppermute(same[NH // 2 :], ("zh", "zl"), [(k, (k - 1) % NZ) for k in range(NZ)])
    update = call(update_kernel, (N, WIDTH), [VMEM_SPEC] * 3)(
        mixer_input, input_map, log_decay.T
    )
    update = call(cut_kernel, (NCTX, PIECE_ROWS, PIECE_COLS), [VMEM_SPEC, ANY_SPEC])(update, same)
    update = lax.all_to_all(update, ("cx", "zh", "zl"), 0, 0)
    bufs = [
        pltpu.VMEM((NX * KEYS, 256), BF16),
        pltpu.VMEM((DH + 16, NX * KEYS), BF16),
        pltpu.VMEM((256, QUERIES), BF16),
    ]
    total, top = pl.pallas_call(
        attend_same_kernel,
        out_shape=[
            jax.ShapeDtypeStruct((NX, DH + 16, QUERIES), F32),
            jax.ShapeDtypeStruct((NX, 1, QUERIES), F32),
        ],
        in_specs=[SMEM_SPEC, VMEM_SPEC, VMEM_SPEC],
        out_specs=[VMEM_SPEC, VMEM_SPEC],
        scratch_shapes=bufs,
        compiler_params=pltpu.CompilerParams(vmem_limit_bytes=24 << 20),
    )(place_zx, packed, same)
    prefix = call(prefix_kernel, (NCTX, PIECE_ROWS, PIECE_COLS), [SMEM_SPEC] + [VMEM_SPEC] * 5)(
        place, update, same, below, above, top
    )
    entering = lax.all_to_all(prefix, ("cx", "zh", "zl"), 0, 0)
    attended = pl.pallas_call(
        attend_other_kernel,
        out_shape=[jax.ShapeDtypeStruct((GDH, T), BF16)] * NX,
        in_specs=[SMEM_SPEC] + [VMEM_SPEC] * 5 + [ANY_SPEC],
        out_specs=[VMEM_SPEC] * NX,
        scratch_shapes=bufs,
        compiler_params=pltpu.CompilerParams(vmem_limit_bytes=24 << 20),
    )(place_zx, packed, below, above, total, top, prefix)
    attended = [attended[0]] + [
        lax.ppermute(attended[s], "cx", [(k, (k + s) % NX) for k in range(NX)])
        for s in range(1, NX)
    ]
    mixer_output, end = pl.pallas_call(
        mix_kernel,
        out_shape=[
            jax.ShapeDtypeStruct((T, WIDTH), BF16),
            jax.ShapeDtypeStruct((8, 128), F32),
        ],
        in_specs=[VMEM_SPEC] * 5,
        out_specs=[VMEM_SPEC] * 2,
        compiler_params=pltpu.CompilerParams(vmem_limit_bytes=12 << 20),
    )(mixer_input, input_map, output_map, log_decay.T, entering)
    attention_output = call(
        place_kernel, (T, QH * DH), [SMEM_SPEC] + [VMEM_SPEC] * (NX + 1)
    )(place_zx, *attended, end)
    return mixer_output, attention_output


def solution(mesh):
    grid = Mesh(mesh.devices.reshape(-1, NX, NH, 2), ("dp", "cx", "zh", "zl"))
    spec = P(("dp", "cx", "zh", "zl"), None)
    return jax.shard_map(
        per_device,
        mesh=grid,
        in_specs=(spec,) * 7,
        out_specs=(spec, spec),
        check_vma=False,
    )
```

```python
import math

import jax
import jax.numpy as jnp
from jax import lax
from jax.experimental import pallas as pl
from jax.experimental.pallas import tpu as pltpu
from jax.sharding import Mesh
from jax.sharding import PartitionSpec as P

MIXER_HEADS = 40
P_SIZE = 64
N = 128
QH = 32
KVH = 4
DH = 80
T = 128
WIDTH = MIXER_HEADS * P_SIZE
GROUP = QH // KVH
GDH = GROUP * DH
NX = 4
NH = 4
NZ = 2 * NH
NCTX = NX * NZ
PIECE_ROWS = 16
PIECE_COLS = 640
masked_score = -1e30
F32 = jnp.float32
BF16 = jnp.bfloat16


def split2(a):
    hi = a.astype(BF16)
    return hi, (a - hi.astype(F32)).astype(BF16)


def dot(a, b):
    return jnp.dot(a, b, preferred_element_type=F32)


def dot_nt(a, b):
    return lax.dot_general(a, b, (((1,), (1,)), ((), ())), preferred_element_type=F32)


def head_spread():
    rows = lax.broadcasted_iota(jnp.int32, (MIXER_HEADS, WIDTH), 0)
    cols = lax.broadcasted_iota(jnp.int32, (MIXER_HEADS, WIDTH), 1)
    return jnp.where(cols // P_SIZE == rows, 1.0, 0.0).astype(BF16)


def spread(a, onehot):
    hi, lo = split2(a)
    return dot(hi, onehot) + dot(lo, onehot)


def cumulative_of(decay):
    rows = lax.broadcasted_iota(jnp.int32, (T, T), 0)
    cols = lax.broadcasted_iota(jnp.int32, (T, T), 1)
    lower = jnp.where(cols <= rows, 1.0, 0.0).astype(F32)
    return lax.dot_general(
        lower,
        decay,
        (((1,), (1,)), ((), ())),
        precision=lax.Precision.HIGHEST,
        preferred_element_type=F32,
    )


def update_kernel(x_ref, in_ref, decay_ref, out_ref):
    cumulative = cumulative_of(decay_ref[...])
    last = cumulative[T - 1 : T, :]
    tail = spread(jnp.exp(last - cumulative), head_spread())
    hi, lo = split2(x_ref[...].astype(F32) * tail)
    in_t = in_ref[...].astype(F32).T.astype(BF16)
    out_ref[...] = (dot(in_t, hi) + dot(in_t, lo)).astype(BF16)


def cut_kernel(in_ref, after_ref, out_ref):
    across = WIDTH // PIECE_COLS
    for i in range(N // PIECE_ROWS):
        for j in range(across):
            out_ref[i * across + j] = in_ref[
                i * PIECE_ROWS : (i + 1) * PIECE_ROWS, j * PIECE_COLS : (j + 1) * PIECE_COLS
            ]


def prefix_kernel(place_ref, in_ref, same_ref, below_ref, above_ref, after_ref, out_ref):
    first_head = (place_ref[0] % (WIDTH // PIECE_COLS)) * (PIECE_COLS // P_SIZE)
    parity = place_ref[0] % 2
    lane = lax.broadcasted_iota(jnp.int32, (128, PIECE_COLS), 0)
    cols = lax.broadcasted_iota(jnp.int32, (128, PIECE_COLS), 1)
    head = first_head + cols // P_SIZE
    onehot = jnp.where((lane == head) | (lane == head + 64), 1.0, 0.0).astype(BF16)
    state = jnp.zeros((PIECE_ROWS, PIECE_COLS), F32)
    half = NH // 2
    for k in range(NCTX):
        out_ref[k] = state.astype(BF16)
        c, i = k // NZ, k % NZ // 2
        mine = same_ref[i, c, 2 * DH :, :].astype(F32)
        other = below_ref[i, c, 2 * DH :, :] if i < half else above_ref[i - half, c, 2 * DH :, :]
        decay = jnp.where(parity == k % 2, mine, other.astype(F32)).astype(BF16)
        state = dot(decay, onehot) * state + in_ref[k].astype(F32)


def mix_kernel(x_ref, in_ref, map_ref, decay_ref, enter_ref, out_ref, end_ref):
    end_ref[...] = jnp.zeros(end_ref.shape, F32)
    cumulative = cumulative_of(decay_ref[...])
    middle = 0.5 * cumulative[T - 1 : T, :]
    onehot = head_spread()
    ahead = spread(jnp.exp(cumulative - middle), onehot)
    behind = spread(jnp.exp(middle - cumulative), onehot)
    start = spread(jnp.exp(jnp.broadcast_to(middle, (8, MIXER_HEADS))), onehot)[0:1, :]
    hi, lo = split2(x_ref[...].astype(F32) * behind)
    out_map = map_ref[...]
    match = dot_nt(out_map, in_ref[...])
    rows = lax.broadcasted_iota(jnp.int32, (T, T), 0)
    cols = lax.broadcasted_iota(jnp.int32, (T, T), 1)
    match_hi, match_lo = split2(jnp.where(cols <= rows, match, 0.0))
    inner = dot(match_hi, hi) + dot(match_hi, lo) + dot(match_lo, hi)
    for j in range(WIDTH // PIECE_COLS):
        cut = slice(j * PIECE_COLS, (j + 1) * PIECE_COLS)
        entering = jnp.concatenate(
            [enter_ref[i * (WIDTH // PIECE_COLS) + j] for i in range(N // PIECE_ROWS)], axis=0
        )
        carried = dot(out_map, entering)
        out_ref[:, cut] = (ahead[:, cut] * (inner[:, cut] + start[:, cut] * carried)).astype(BF16)


QUERIES = GROUP * T
KEYS = NH * T


def pack_kernel(q_hbm, k_hbm, v_hbm, decay_hbm, out_ref, q_ref, k_ref, v_ref, decay_ref, sems):
    copies = [
        pltpu.make_async_copy(decay_hbm, decay_ref, sems.at[0]),
        pltpu.make_async_copy(k_hbm, k_ref, sems.at[1]),
        pltpu.make_async_copy(v_hbm, v_ref, sems.at[2]),
        pltpu.make_async_copy(q_hbm, q_ref, sems.at[3]),
    ]
    for copy in copies:
        copy.start()
    for copy in copies:
        copy.wait()
    total = lax.dot_general(
        jnp.ones((PIECE_ROWS, T), F32),
        decay_ref[...],
        (((1,), (1,)), ((), ())),
        precision=lax.Precision.HIGHEST,
        preferred_element_type=F32,
    )
    total_hi, total_lo = split2(jnp.exp(total))
    head = lax.broadcasted_iota(jnp.int32, (MIXER_HEADS, 128), 0)
    lane = lax.broadcasted_iota(jnp.int32, (MIXER_HEADS, 128), 1)
    place_hi = jnp.where(lane == head, 1.0, 0.0).astype(BF16)
    place_lo = jnp.where(lane == head + 64, 1.0, 0.0).astype(BF16)
    decay = (dot(total_hi, place_hi) + dot(total_lo, place_lo)).astype(BF16)
    for g in range(KVH):
        q = q_ref[:, g * GDH : (g + 1) * GDH].astype(F32)
        out_ref[g, :GDH, :] = q.T.astype(BF16)
        out_ref[g, GDH : GDH + DH, :] = k_ref[g * DH : (g + 1) * DH, :]
        out_ref[g, GDH + DH : GDH + 2 * DH, :] = v_ref[g * DH : (g + 1) * DH, :]
        out_ref[g, GDH + 2 * DH :, :] = decay


def attend(place_ref, q_ref, block, parity, k_buf, v_buf, q_buf, begin, end):
    z = place_ref[0]
    scale = math.log2(math.e) / math.sqrt(DH)
    row = lax.broadcasted_iota(jnp.int32, (KEYS, QUERIES), 0)
    row = row + row // T * T + parity * T
    col = lax.broadcasted_iota(jnp.int32, (KEYS, QUERIES), 1) % T
    ones = jnp.where(lax.broadcasted_iota(jnp.int32, (16, KEYS), 0) == 0, 1.0, 0.0).astype(BF16)
    blank = jnp.zeros((128 - DH, T), F32)
    blank_q = jnp.zeros((128 - DH, QUERIES), BF16)
    for c in range(NX):
        q_buf[DH:128, :] = blank_q
        q_buf[128 + DH :, :] = blank_q
        for h in range(GROUP):
            hi, lo = split2(q_ref[c, h * DH : (h + 1) * DH, :].astype(F32) * scale)
            q_buf[:DH, h * T : (h + 1) * T] = hi
            q_buf[128 : 128 + DH, h * T : (h + 1) * T] = lo
        v_buf[DH:, c * KEYS : (c + 1) * KEYS] = ones
        for i in range(NH):
            at = slice(c * KEYS + i * T, c * KEYS + (i + 1) * T)
            kv = block(c, i)
            v_buf[:DH, at] = kv[DH : 2 * DH, :]
            k = jnp.concatenate([kv[:DH, :].astype(F32), blank], axis=0).T.astype(BF16)
            k_buf[at, :128] = k
            k_buf[at, 128:] = k
        q = q_buf[...]

        def scores(j, c=c, q=q):
            found = dot(k_buf[j * KEYS : (j + 1) * KEYS, :], q)
            if j == c:
                found = jnp.where(row <= col + z * T, found, masked_score)
            return found

        total, top = begin(c)
        found = scores(0)
        for j in range(c + 1):
            later = scores(j + 1) if j < c else None
            highest = jnp.max(found, axis=0, keepdims=True)
            if top is None:
                top = highest
            else:
                raised = jnp.maximum(top, highest)
                total = total * jnp.exp2(top - raised)
                top = raised
            expos = jnp.exp2(found - top).astype(BF16)
            summed = dot(v_buf[:, j * KEYS : (j + 1) * KEYS], expos)
            total = summed if total is None else total + summed
            found = later
        end(c, total, top)


def attend_same_kernel(place_ref, q_ref, same_ref, total_ref, top_ref, *bufs):
    def end(c, total, top):
        total_ref[c] = total
        top_ref[c] = top

    attend(
        place_ref,
        q_ref,
        lambda c, i: same_ref[i, c],
        place_ref[0] % 2,
        *bufs,
        lambda c: (None, None),
        end,
    )


def attend_other_kernel(
    place_ref, q_ref, below_ref, above_ref, total_ref, top_ref, after_ref, *refs
):
    out_refs, bufs = refs[:NX], refs[NX:]

    def end(c, total, top):
        done = (total[:DH, :] / total[DH : DH + 1, :]).astype(BF16)
        step = lax.rem(c + NX - place_ref[1], NX)
        for s in range(NX):

            @pl.when(step == s)
            def _(out_ref=out_refs[s]):
                for h in range(GROUP):
                    out_ref[h * DH : (h + 1) * DH, :] = done[:, h * T : (h + 1) * T]

    half = NH // 2
    attend(
        place_ref,
        q_ref,
        lambda c, i: below_ref[i, c] if i < half else above_ref[i - half, c],
        1 - place_ref[0] % 2,
        *bufs,
        lambda c: (total_ref[c], top_ref[c]),
        end,
    )


def place_kernel(place_ref, *refs):
    out_ref = refs[-1]
    for s in range(NX):
        g = lax.rem(place_ref[1] + (NX - s), NX)
        cols = pl.ds(pl.multiple_of(g * GDH, 128), GDH)
        out_ref[:, cols] = refs[s][...].astype(F32).T.astype(BF16)


VMEM_SPEC = pl.BlockSpec(memory_space=pltpu.VMEM)
SMEM_SPEC = pl.BlockSpec(memory_space=pltpu.SMEM)
ANY_SPEC = pl.BlockSpec(memory_space=pl.ANY)
HBM_SPEC = pl.BlockSpec(memory_space=pltpu.HBM)
PACK_BUFS = [
    pltpu.VMEM((T, QH * DH), BF16),
    pltpu.VMEM((KVH * DH, T), BF16),
    pltpu.VMEM((KVH * DH, T), BF16),
    pltpu.VMEM((MIXER_HEADS, T), F32),
    pltpu.SemaphoreType.DMA((4,)),
]


def call(kernel, shape, specs, scratch=(), limit=12):
    return pl.pallas_call(
        kernel,
        out_shape=jax.ShapeDtypeStruct(shape, BF16),
        in_specs=specs,
        out_specs=VMEM_SPEC,
        scratch_shapes=list(scratch),
        compiler_params=pltpu.CompilerParams(vmem_limit_bytes=limit << 20),
    )


def per_device(mixer_input, input_map, output_map, log_decay, query_rows, key_rows, value_rows):
    place_zx = jnp.stack([lax.axis_index(("zh", "zl")), lax.axis_index("cx")]).astype(jnp.int32)
    place = lax.axis_index(("cx", "zh", "zl")).astype(jnp.int32).reshape(1)
    packed = call(pack_kernel, (KVH, GDH + 2 * DH + PIECE_ROWS, T), [HBM_SPEC] * 4, PACK_BUFS, 62)(
        query_rows, key_rows.T, value_rows.T, log_decay.T
    )
    packed = lax.all_to_all(packed, "cx", 0, 0)
    same = lax.all_gather(packed[:, GDH:, :], "zh")
    below = lax.ppermute(same[: NH // 2], ("zh", "zl"), [(k, (k + 1) % NZ) for k in range(NZ)])
    above = lax.ppermute(same[NH // 2 :], ("zh", "zl"), [(k, (k - 1) % NZ) for k in range(NZ)])
    update = call(update_kernel, (N, WIDTH), [VMEM_SPEC] * 3)(
        mixer_input, input_map, log_decay.T
    )
    update = call(cut_kernel, (NCTX, PIECE_ROWS, PIECE_COLS), [VMEM_SPEC, ANY_SPEC])(update, same)
    update = lax.all_to_all(update, ("cx", "zh", "zl"), 0, 0)
    bufs = [
        pltpu.VMEM((NX * KEYS, 256), BF16),
        pltpu.VMEM((DH + 16, NX * KEYS), BF16),
        pltpu.VMEM((256, QUERIES), BF16),
    ]
    total, top = pl.pallas_call(
        attend_same_kernel,
        out_shape=[
            jax.ShapeDtypeStruct((NX, DH + 16, QUERIES), F32),
            jax.ShapeDtypeStruct((NX, 1, QUERIES), F32),
        ],
        in_specs=[SMEM_SPEC, VMEM_SPEC, VMEM_SPEC],
        out_specs=[VMEM_SPEC, VMEM_SPEC],
        scratch_shapes=bufs,
        compiler_params=pltpu.CompilerParams(vmem_limit_bytes=24 << 20),
    )(place_zx, packed, same)
    prefix = call(prefix_kernel, (NCTX, PIECE_ROWS, PIECE_COLS), [SMEM_SPEC] + [VMEM_SPEC] * 5)(
        place, update, same, below, above, top
    )
    entering = lax.all_to_all(prefix, ("cx", "zh", "zl"), 0, 0)
    attended = pl.pallas_call(
        attend_other_kernel,
        out_shape=[jax.ShapeDtypeStruct((GDH, T), BF16)] * NX,
        in_specs=[SMEM_SPEC] + [VMEM_SPEC] * 5 + [ANY_SPEC],
        out_specs=[VMEM_SPEC] * NX,
        scratch_shapes=bufs,
        compiler_params=pltpu.CompilerParams(vmem_limit_bytes=24 << 20),
    )(place_zx, packed, below, above, total, top, prefix)
    attended = [attended[0]] + [
        lax.ppermute(attended[s], "cx", [(k, (k + s) % NX) for k in range(NX)])
        for s in range(1, NX)
    ]
    mixer_output, end = pl.pallas_call(
        mix_kernel,
        out_shape=[
            jax.ShapeDtypeStruct((T, WIDTH), BF16),
            jax.ShapeDtypeStruct((8, 128), F32),
        ],
        in_specs=[VMEM_SPEC] * 5,
        out_specs=[VMEM_SPEC] * 2,
        compiler_params=pltpu.CompilerParams(vmem_limit_bytes=12 << 20),
    )(mixer_input, input_map, output_map, log_decay.T, entering)
    attention_output = call(
        place_kernel, (T, QH * DH), [SMEM_SPEC] + [VMEM_SPEC] * (NX + 1)
    )(place_zx, *attended, end)
    return mixer_output, attention_output


def solution(mesh):
    grid = Mesh(mesh.devices.reshape(-1, NX, NH, 2), ("dp", "cx", "zh", "zl"))
    spec = P(("dp", "cx", "zh", "zl"), None)
    return jax.shard_map(
        per_device,
        mesh=grid,
        in_specs=(spec,) * 7,
        out_specs=(spec, spec),
        check_vma=False,
    )
```

```python
import math

import jax
import jax.numpy as jnp
from jax import lax
from jax.experimental import pallas as pl
from jax.experimental.pallas import tpu as pltpu
from jax.sharding import Mesh
from jax.sharding import PartitionSpec as P

MIXER_HEADS = 40
P_SIZE = 64
N = 128
QH = 32
KVH = 4
DH = 80
T = 128
WIDTH = MIXER_HEADS * P_SIZE
GROUP = QH // KVH
GDH = GROUP * DH
NX = 4
NH = 4
NZ = 2 * NH
NCTX = NX * NZ
PIECE_ROWS = 16
PIECE_COLS = 640
masked_score = -1e30
F32 = jnp.float32
BF16 = jnp.bfloat16


def split2(a):
    hi = a.astype(BF16)
    return hi, (a - hi.astype(F32)).astype(BF16)


def dot(a, b):
    return jnp.dot(a, b, preferred_element_type=F32)


def dot_nt(a, b):
    return lax.dot_general(a, b, (((1,), (1,)), ((), ())), preferred_element_type=F32)


def head_spread():
    rows = lax.broadcasted_iota(jnp.int32, (MIXER_HEADS, WIDTH), 0)
    cols = lax.broadcasted_iota(jnp.int32, (MIXER_HEADS, WIDTH), 1)
    return jnp.where(cols // P_SIZE == rows, 1.0, 0.0).astype(BF16)


def spread(a, onehot):
    hi, lo = split2(a)
    return dot(hi, onehot) + dot(lo, onehot)


def cumulative_of(decay):
    rows = lax.broadcasted_iota(jnp.int32, (T, T), 0)
    cols = lax.broadcasted_iota(jnp.int32, (T, T), 1)
    lower = jnp.where(cols <= rows, 1.0, 0.0).astype(F32)
    return lax.dot_general(
        lower,
        decay,
        (((1,), (1,)), ((), ())),
        precision=lax.Precision.HIGHEST,
        preferred_element_type=F32,
    )


def update_kernel(x_ref, in_ref, decay_ref, out_ref):
    cumulative = cumulative_of(decay_ref[...])
    last = cumulative[T - 1 : T, :]
    tail = spread(jnp.exp(last - cumulative), head_spread())
    hi, lo = split2(x_ref[...].astype(F32) * tail)
    in_t = in_ref[...].astype(F32).T.astype(BF16)
    out_ref[...] = (dot(in_t, hi) + dot(in_t, lo)).astype(BF16)


def cut_kernel(in_ref, after_ref, out_ref):
    across = WIDTH // PIECE_COLS
    for i in range(N // PIECE_ROWS):
        for j in range(across):
            out_ref[i * across + j] = in_ref[
                i * PIECE_ROWS : (i + 1) * PIECE_ROWS, j * PIECE_COLS : (j + 1) * PIECE_COLS
            ]


def prefix_kernel(place_ref, in_ref, same_ref, below_ref, above_ref, after_ref, out_ref):
    first_head = (place_ref[0] % (WIDTH // PIECE_COLS)) * (PIECE_COLS // P_SIZE)
    parity = place_ref[0] % 2
    lane = lax.broadcasted_iota(jnp.int32, (128, PIECE_COLS), 0)
    cols = lax.broadcasted_iota(jnp.int32, (128, PIECE_COLS), 1)
    head = first_head + cols // P_SIZE
    onehot = jnp.where((lane == head) | (lane == head + 64), 1.0, 0.0).astype(BF16)
    state = jnp.zeros((PIECE_ROWS, PIECE_COLS), F32)
    half = NH // 2
    for k in range(NCTX):
        out_ref[k] = state.astype(BF16)
        c, i = k // NZ, k % NZ // 2
        mine = same_ref[i, c, 2 * DH :, :].astype(F32)
        other = below_ref[i, c, 2 * DH :, :] if i < half else above_ref[i - half, c, 2 * DH :, :]
        decay = jnp.where(parity == k % 2, mine, other.astype(F32)).astype(BF16)
        state = dot(decay, onehot) * state + in_ref[k].astype(F32)


def mix_kernel(x_ref, in_ref, map_ref, decay_ref, enter_ref, out_ref, end_ref):
    end_ref[...] = jnp.zeros(end_ref.shape, F32)
    cumulative = cumulative_of(decay_ref[...])
    middle = 0.5 * cumulative[T - 1 : T, :]
    onehot = head_spread()
    ahead = spread(jnp.exp(cumulative - middle), onehot)
    behind = spread(jnp.exp(middle - cumulative), onehot)
    start = spread(jnp.exp(jnp.broadcast_to(middle, (8, MIXER_HEADS))), onehot)[0:1, :]
    hi, lo = split2(x_ref[...].astype(F32) * behind)
    out_map = map_ref[...]
    match = dot_nt(out_map, in_ref[...])
    rows = lax.broadcasted_iota(jnp.int32, (T, T), 0)
    cols = lax.broadcasted_iota(jnp.int32, (T, T), 1)
    match_hi, match_lo = split2(jnp.where(cols <= rows, match, 0.0))
    inner = dot(match_hi, hi) + dot(match_hi, lo) + dot(match_lo, hi)
    for j in range(WIDTH // PIECE_COLS):
        cut = slice(j * PIECE_COLS, (j + 1) * PIECE_COLS)
        entering = jnp.concatenate(
            [enter_ref[i * (WIDTH // PIECE_COLS) + j] for i in range(N // PIECE_ROWS)], axis=0
        )
        carried = dot(out_map, entering)
        out_ref[:, cut] = (ahead[:, cut] * (inner[:, cut] + start[:, cut] * carried)).astype(BF16)


QUERIES = GROUP * T
KEYS = NH * T


def pack_kernel(q_hbm, k_hbm, v_hbm, decay_hbm, out_ref, q_ref, k_ref, v_ref, decay_ref, sems):
    copies = [
        pltpu.make_async_copy(decay_hbm, decay_ref, sems.at[0]),
        pltpu.make_async_copy(k_hbm, k_ref, sems.at[1]),
        pltpu.make_async_copy(v_hbm, v_ref, sems.at[2]),
        pltpu.make_async_copy(q_hbm, q_ref, sems.at[3]),
    ]
    for copy in copies:
        copy.start()
    for copy in copies:
        copy.wait()
    total = lax.dot_general(
        jnp.ones((PIECE_ROWS, T), F32),
        decay_ref[...],
        (((1,), (1,)), ((), ())),
        precision=lax.Precision.HIGHEST,
        preferred_element_type=F32,
    )
    total_hi, total_lo = split2(jnp.exp(total))
    head = lax.broadcasted_iota(jnp.int32, (MIXER_HEADS, 128), 0)
    lane = lax.broadcasted_iota(jnp.int32, (MIXER_HEADS, 128), 1)
    place_hi = jnp.where(lane == head, 1.0, 0.0).astype(BF16)
    place_lo = jnp.where(lane == head + 64, 1.0, 0.0).astype(BF16)
    decay = (dot(total_hi, place_hi) + dot(total_lo, place_lo)).astype(BF16)
    for g in range(KVH):
        q = q_ref[:, g * GDH : (g + 1) * GDH].astype(F32)
        out_ref[g, :GDH, :] = q.T.astype(BF16)
        out_ref[g, GDH : GDH + DH, :] = k_ref[g * DH : (g + 1) * DH, :]
        out_ref[g, GDH + DH : GDH + 2 * DH, :] = v_ref[g * DH : (g + 1) * DH, :]
        out_ref[g, GDH + 2 * DH :, :] = decay


def attend(place_ref, q_ref, block, parity, k_buf, v_buf, q_buf, begin, end):
    z = place_ref[0]
    scale = math.log2(math.e) / math.sqrt(DH)
    row = lax.broadcasted_iota(jnp.int32, (KEYS, QUERIES), 0)
    row = row + row // T * T + parity * T
    col = lax.broadcasted_iota(jnp.int32, (KEYS, QUERIES), 1) % T
    ones = jnp.where(lax.broadcasted_iota(jnp.int32, (16, KEYS), 0) == 0, 1.0, 0.0).astype(BF16)
    blank = jnp.zeros((128 - DH, T), F32)
    blank_q = jnp.zeros((128 - DH, QUERIES), BF16)
    for c in range(NX):
        q_buf[DH:128, :] = blank_q
        q_buf[128 + DH :, :] = blank_q
        for h in range(GROUP):
            hi, lo = split2(q_ref[c, h * DH : (h + 1) * DH, :].astype(F32) * scale)
            q_buf[:DH, h * T : (h + 1) * T] = hi
            q_buf[128 : 128 + DH, h * T : (h + 1) * T] = lo
        v_buf[DH:, c * KEYS : (c + 1) * KEYS] = ones
        for i in range(NH):
            at = slice(c * KEYS + i * T, c * KEYS + (i + 1) * T)
            kv = block(c, i)
            v_buf[:DH, at] = kv[DH : 2 * DH, :]
            k = jnp.concatenate([kv[:DH, :].astype(F32), blank], axis=0).T.astype(BF16)
            k_buf[at, :128] = k
            k_buf[at, 128:] = k
        q = q_buf[...]

        def scores(j, c=c, q=q):
            found = dot(k_buf[j * KEYS : (j + 1) * KEYS, :], q)
            if j == c:
                found = jnp.where(row <= col + z * T, found, masked_score)
            return found

        total, top = begin(c)
        found = scores(0)
        for j in range(c + 1):
            later = scores(j + 1) if j < c else None
            highest = jnp.max(found, axis=0, keepdims=True)
            if top is None:
                top = highest
            else:
                raised = jnp.maximum(top, highest)
                total = total * jnp.exp2(top - raised)
                top = raised
            expos = jnp.exp2(found - top).astype(BF16)
            summed = dot(v_buf[:, j * KEYS : (j + 1) * KEYS], expos)
            total = summed if total is None else total + summed
            found = later
        end(c, total, top)


def attend_same_kernel(place_ref, q_ref, same_ref, total_ref, top_ref, *bufs):
    def end(c, total, top):
        total_ref[c] = total
        top_ref[c] = top

    attend(
        place_ref,
        q_ref,
        lambda c, i: same_ref[i, c],
        place_ref[0] % 2,
        *bufs,
        lambda c: (None, None),
        end,
    )


def attend_other_kernel(
    place_ref, q_ref, below_ref, above_ref, total_ref, top_ref, after_ref, *refs
):
    out_refs, bufs, total_buf, sems = refs[:NX], refs[NX:-2], refs[-2], refs[-1]
    copies = [
        pltpu.make_async_copy(total_ref.at[c], total_buf.at[c], sems.at[c]) for c in range(NX)
    ]
    for copy in copies:
        copy.start()

    def begin(c):
        copies[c].wait()
        return total_buf[c], top_ref[c]


    def end(c, total, top):
        done = (total[:DH, :] / total[DH : DH + 1, :]).astype(BF16)
        step = lax.rem(c + NX - place_ref[1], NX)
        for s in range(NX):

            @pl.when(step == s)
            def _(out_ref=out_refs[s]):
                for h in range(GROUP):
                    out_ref[h * DH : (h + 1) * DH, :] = done[:, h * T : (h + 1) * T]

    half = NH // 2
    attend(
        place_ref,
        q_ref,
        lambda c, i: below_ref[i, c] if i < half else above_ref[i - half, c],
        1 - place_ref[0] % 2,
        *bufs,
        begin,
        end,
    )


def place_kernel(place_ref, *refs):
    out_ref = refs[-1]
    for s in range(NX):
        g = lax.rem(place_ref[1] + (NX - s), NX)
        cols = pl.ds(pl.multiple_of(g * GDH, 128), GDH)
        out_ref[:, cols] = refs[s][...].astype(F32).T.astype(BF16)


VMEM_SPEC = pl.BlockSpec(memory_space=pltpu.VMEM)
SMEM_SPEC = pl.BlockSpec(memory_space=pltpu.SMEM)
ANY_SPEC = pl.BlockSpec(memory_space=pl.ANY)
HBM_SPEC = pl.BlockSpec(memory_space=pltpu.HBM)
PACK_BUFS = [
    pltpu.VMEM((T, QH * DH), BF16),
    pltpu.VMEM((KVH * DH, T), BF16),
    pltpu.VMEM((KVH * DH, T), BF16),
    pltpu.VMEM((MIXER_HEADS, T), F32),
    pltpu.SemaphoreType.DMA((4,)),
]


def call(kernel, shape, specs, scratch=(), limit=12):
    return pl.pallas_call(
        kernel,
        out_shape=jax.ShapeDtypeStruct(shape, BF16),
        in_specs=specs,
        out_specs=VMEM_SPEC,
        scratch_shapes=list(scratch),
        compiler_params=pltpu.CompilerParams(vmem_limit_bytes=limit << 20),
    )


def per_device(mixer_input, input_map, output_map, log_decay, query_rows, key_rows, value_rows):
    place_zx = jnp.stack([lax.axis_index(("zh", "zl")), lax.axis_index("cx")]).astype(jnp.int32)
    place = lax.axis_index(("cx", "zh", "zl")).astype(jnp.int32).reshape(1)
    packed = call(pack_kernel, (KVH, GDH + 2 * DH + PIECE_ROWS, T), [HBM_SPEC] * 4, PACK_BUFS, 62)(
        query_rows, key_rows.T, value_rows.T, log_decay.T
    )
    packed = lax.all_to_all(packed, "cx", 0, 0)
    same = lax.all_gather(packed[:, GDH:, :], "zh")
    below = lax.ppermute(same[: NH // 2], ("zh", "zl"), [(k, (k + 1) % NZ) for k in range(NZ)])
    above = lax.ppermute(same[NH // 2 :], ("zh", "zl"), [(k, (k - 1) % NZ) for k in range(NZ)])
    update = call(update_kernel, (N, WIDTH), [VMEM_SPEC] * 3)(
        mixer_input, input_map, log_decay.T
    )
    update = call(cut_kernel, (NCTX, PIECE_ROWS, PIECE_COLS), [VMEM_SPEC, ANY_SPEC])(update, same)
    update = lax.all_to_all(update, ("cx", "zh", "zl"), 0, 0)
    bufs = [
        pltpu.VMEM((NX * KEYS, 256), BF16),
        pltpu.VMEM((DH + 16, NX * KEYS), BF16),
        pltpu.VMEM((256, QUERIES), BF16),
    ]
    total, top = pl.pallas_call(
        attend_same_kernel,
        out_shape=[
            jax.ShapeDtypeStruct((NX, DH + 16, QUERIES), F32),
            jax.ShapeDtypeStruct((NX, 1, QUERIES), F32),
        ],
        in_specs=[SMEM_SPEC, VMEM_SPEC, VMEM_SPEC],
        out_specs=[VMEM_SPEC, VMEM_SPEC],
        scratch_shapes=bufs,
        compiler_params=pltpu.CompilerParams(vmem_limit_bytes=24 << 20),
    )(place_zx, packed, same)
    prefix = call(prefix_kernel, (NCTX, PIECE_ROWS, PIECE_COLS), [SMEM_SPEC] + [VMEM_SPEC] * 5)(
        place, update, same, below, above, top
    )
    entering = lax.all_to_all(prefix, ("cx", "zh", "zl"), 0, 0)
    attended = pl.pallas_call(
        attend_other_kernel,
        out_shape=[jax.ShapeDtypeStruct((GDH, T), BF16)] * NX,
        in_specs=[SMEM_SPEC] + [VMEM_SPEC] * 3 + [HBM_SPEC, VMEM_SPEC, ANY_SPEC],
        out_specs=[VMEM_SPEC] * NX,
        scratch_shapes=bufs
        + [
            pltpu.VMEM((NX, DH + 16, QUERIES), F32),
            pltpu.SemaphoreType.DMA((NX,)),
        ],
        compiler_params=pltpu.CompilerParams(vmem_limit_bytes=56 << 20),
    )(place_zx, packed, below, above, total, top, prefix)
    attended = [attended[0]] + [
        lax.ppermute(attended[s], "cx", [(k, (k + s) % NX) for k in range(NX)])
        for s in range(1, NX)
    ]
    mixer_output, end = pl.pallas_call(
        mix_kernel,
        out_shape=[
            jax.ShapeDtypeStruct((T, WIDTH), BF16),
            jax.ShapeDtypeStruct((8, 128), F32),
        ],
        in_specs=[VMEM_SPEC] * 5,
        out_specs=[VMEM_SPEC] * 2,
        compiler_params=pltpu.CompilerParams(vmem_limit_bytes=12 << 20),
    )(mixer_input, input_map, output_map, log_decay.T, entering)
    attention_output = call(
        place_kernel, (T, QH * DH), [SMEM_SPEC] + [VMEM_SPEC] * (NX + 1)
    )(place_zx, *attended, end)
    return mixer_output, attention_output


def solution(mesh):
    grid = Mesh(mesh.devices.reshape(-1, NX, NH, 2), ("dp", "cx", "zh", "zl"))
    spec = P(("dp", "cx", "zh", "zl"), None)
    return jax.shard_map(
        per_device,
        mesh=grid,
        in_specs=(spec,) * 7,
        out_specs=(spec, spec),
        check_vma=False,
    )
```
